256 devices in a mesh: grp: 16 (over y_hi, x, core), tp: 16 (over y_lo, z).
Axes of the slice: x: 4, y: 4 (y_hi: 2, y_lo: 2; y = y_hi * 2 + y_lo), z: 8, core: 2. Of those that a mesh axis runs over, the one named last changes fastest.
Arguments:
- x_rows: bfloat16 [16384, 4096], P(('grp', 'tp')), may hold values from -6 to 6
- norm_gain: float32 [4096], replicated, may hold values from 0.1 to 1.9
- w_query: bfloat16 [4096, 4096], P(None, 'tp'), may hold values from -0.25 to 0.25
- w_keyval: bfloat16 [4096, 2, 1024], P(None, None, 'tp'), may hold values from -0.09375 to 0.09375
- w_out: bfloat16 [4096, 4096], P('tp'), may hold values from -0.75 to 0.75
- prefix_cache: bfloat16 [32, 128, 2, 1024], P('grp', None, None, 'tp'), may hold values from -70 to 70, as said below
- page_table: int32 [32], replicated, may hold values from 0 to 31, each once
- request_ids: int32 [16384], replicated, may hold values from 0 to 31, never falling along the last dimension, each value on 1 to 1024 neighbouring positions
Outputs:
- attn_out: bfloat16 [16384, 4096], P(('grp', 'tp'))
The draws below stay inside these ranges and needn't reach their ends.
Inputs may be any that keep to these rules, and one draw needn't show every extreme that they name: `request_ids`: request ids never fall along the stream; each of the 32 requests has 1 to 1024 tokens, one exactly 1024. `page_table`: a permutation; physical page f belongs to group f // 2. `prefix_cache`: keys are stored already rotated for their positions.
All inputs are finite; a program needn't handle non-finite values.
Results may differ from the reference program's by a relative error of at most 0.025.
The reference program's roundings to bfloat16 on the way (of `normed`, `queries`, `keyval`, `keys_new`, `logical`, `weights` and `attn`) count: a program that leaves them out, or rounds other values in their place, can miss the bound.
Values may be sent and summed in bfloat16 or wider, within the bound.
A program may use at most 64 MiB of HBM per device.

```python
import math
import jax
import jax.numpy as jnp
import numpy as np
from jax import lax

D = 4096
H = 32
KVH = 8
HD = 128
PAGE = 128
SINKS = 4
TOK_G = 1024
TOTAL = 16384
PAGES = 32
PREFIX = 4096
WINDOW = 4096
NSEG = 32
N_GRP = 16
N_TP = 16


def draw_prefix_cache(key, part):
    base_key = jax.random.fold_in(key, 11)
    shape = (PAGES, PAGE, 2, KVH * HD)
    base = jnp.clip(jax.random.normal(base_key, shape, jnp.float32), -6.0, 6.0)
    return base.astype(jnp.bfloat16)


def shard_levels(rng, extent, pieces, smallest, high):
    def one(position, shards_of):
        steps = jax.random.uniform(jax.random.fold_in(jax.random.fold_in(rng, 6), position), (shards_of,), jnp.float32, smallest / len(pieces), high / len(pieces))
        return jnp.repeat(jnp.exp(steps), extent[position] // shards_of).reshape((-1,) + (1,) * (len(extent) - position - 1))

    level = one(*pieces[0])
    for cut in pieces[1:]:
        level = level * one(*cut)
    return level


def split_up(count, total, bound, skew):
    loads = [(1 << 20) // math.isqrt(standing ** skew) + 1 for standing in range(2, count + 1)]
    surplus, given = total - bound - (count - 1), [1] * (count - 1)
    while surplus > 0:
        movable = [i for i in range(count - 1) if given[i] < bound]
        whole, budget = sum([loads[i] for i in movable]), surplus
        for i in movable:
            more = min(bound - given[i], max(1, budget * loads[i] // whole), surplus)
            given[i] = given[i] + more
            surplus = surplus - more
    return np.array([bound] + given)


def uneven(rng, number_of, total, most, lean):
    if number_of == 2:
        one = jax.random.randint(rng, (), max(1, total - most), min(most, total - 1) + 1)
        return jnp.stack([one, total - one])
    tallies = jnp.asarray(split_up(number_of, total, most, lean), jnp.int32)
    couples = (number_of - 1) // 2
    giver, taker = tallies[1:1 + 2 * couples:2], tallies[2:2 + 2 * couples:2]
    room = jnp.minimum(giver - 1, most - taker)
    moved = jax.random.randint(jax.random.fold_in(rng, 1), (couples,), 0, 1 << 20) % (room + 1)
    tallies = tallies.at[1:1 + 2 * couples:2].set(giver - moved).at[2:2 + 2 * couples:2].set(taker + moved)
    return tallies[jax.random.permutation(jax.random.fold_in(rng, 2), number_of)]


def scatter_about(own_key, shape, deviation, bound, cuts=(), kind=jnp.bfloat16):
    array = deviation * jax.random.normal(own_key, shape, jnp.float32)
    if cuts:
        array = array * shard_levels(own_key, shape, cuts, -0.22, 0.18)
    return jnp.clip(array, -bound, bound).astype(kind)


def setup_inputs(seed: int = 0) -> dict:
    key_list = jax.random.split(jax.random.key(seed), 9)
    x_rows = scatter_about(key_list[0], (TOTAL, D), 1.0, 6.0, ((0, 256),))
    norm_gain = jnp.clip(1.0 + 0.18 * jax.random.normal(key_list[1], (D,), jnp.float32), 0.1, 1.9)
    w_query = scatter_about(key_list[2], (D, H * HD), (D // 8) ** -0.5, 0.25, ((1, 16),))
    w_keyval = scatter_about(key_list[3], (D, 2, KVH * HD), D ** -0.5, 0.09375, ((2, 16),))
    w_out = scatter_about(key_list[4], (H * HD, D), (H * HD // 64) ** -0.5, 0.75, ((0, 16),))
    prefix_cache = draw_prefix_cache(jax.random.fold_in(key_list[8], 71), 0)
    page_table = jax.random.permutation(key_list[6], PAGES).astype(jnp.int32)
    request_ids = jnp.searchsorted(jnp.cumsum(uneven(key_list[7], NSEG, TOTAL, TOK_G, 2)), jnp.arange(TOTAL), side="right").astype(jnp.int32)
    return {"x_rows": x_rows, "norm_gain": norm_gain, "w_query": w_query, "w_keyval": w_keyval, "w_out": w_out, "prefix_cache": prefix_cache, "page_table": page_table, "request_ids": request_ids}


def settle(values):
    return lax.optimization_barrier(values.astype(jnp.bfloat16))

def rotate(values, positions):
    half = HD // 2
    freqs = 500000.0 ** (-jnp.arange(half, dtype=jnp.float32) * 2.0 / HD)
    angles = positions.astype(jnp.float32)[:, None] * freqs[None, :]
    cosine = jnp.cos(angles)[:, None, :]
    sine = jnp.sin(angles)[:, None, :]
    first = values[..., :half]
    second = values[..., half:]
    return jnp.concatenate([first * cosine - second * sine, second * cosine + first * sine], axis=-1)

def reference(x_rows, norm_gain, w_query, w_keyval, w_out, prefix_cache, page_table, request_ids):
    wide = x_rows.astype(jnp.float32)
    variance = lax.optimization_barrier(jnp.mean(wide * wide, axis=-1, keepdims=True)) + 1e-05
    inverse = lax.rsqrt(variance)
    normed = (wide * inverse * norm_gain).astype(jnp.bfloat16)
    labels = jnp.arange(NSEG, dtype=jnp.int32)
    counts = lax.optimization_barrier(jnp.sum((request_ids[:, None] == labels[None, :]).astype(jnp.int32), axis=0))
    starts = jnp.cumsum(counts) - counts
    stream_index = jnp.arange(TOTAL, dtype=jnp.int32)
    positions = (PREFIX + stream_index - starts[request_ids]).astype(jnp.int32)
    projected = jnp.dot(normed, w_query, preferred_element_type=jnp.float32).reshape(TOTAL, H, HD)
    queries = settle(rotate(projected, positions))
    keyval = settle(jnp.dot(normed, w_keyval.reshape(D, 2 * KVH * HD), preferred_element_type=jnp.float32))
    keyval = keyval.reshape(TOTAL, 2, KVH, HD)
    keys_new = settle(rotate(keyval[:, 0].astype(jnp.float32), positions))
    values_new = keyval[:, 1]
    logical = prefix_cache[page_table].reshape(PREFIX, 2, KVH, HD)
    cache_pos = jnp.arange(PREFIX, dtype=jnp.int32)

    def group_attend(group):
        query_start = (group * TOK_G).astype(jnp.int32)
        suffix_start = (jnp.maximum(group - 1, 0) * TOK_G).astype(jnp.int32)
        group_queries = lax.dynamic_slice_in_dim(queries, query_start, TOK_G, 0).reshape(TOK_G, KVH, H // KVH, HD)
        query_pos = lax.dynamic_slice_in_dim(positions, query_start, TOK_G, 0)
        query_seg = lax.dynamic_slice_in_dim(request_ids, query_start, TOK_G, 0)
        query_index = query_start + jnp.arange(TOK_G, dtype=jnp.int32)
        suffix_keys = lax.dynamic_slice_in_dim(keys_new, suffix_start, 2 * TOK_G, 0)
        suffix_values = lax.dynamic_slice_in_dim(values_new, suffix_start, 2 * TOK_G, 0)
        suffix_pos = lax.dynamic_slice_in_dim(positions, suffix_start, 2 * TOK_G, 0)
        suffix_seg = lax.dynamic_slice_in_dim(request_ids, suffix_start, 2 * TOK_G, 0)
        suffix_index = suffix_start + jnp.arange(2 * TOK_G, dtype=jnp.int32)
        prefix_mask = (cache_pos[None, :] <= query_pos[:, None]) & ((query_pos[:, None] - cache_pos[None, :] < WINDOW) | (cache_pos[None, :] < SINKS))
        suffix_mask = (suffix_seg[None, :] == query_seg[:, None]) & (suffix_index[None, :] <= query_index[:, None])
        suffix_mask = suffix_mask & ((query_pos[:, None] - suffix_pos[None, :] < WINDOW) | (suffix_pos[None, :] < SINKS))
        visible = jnp.concatenate([prefix_mask, suffix_mask], axis=1)
        all_keys = jnp.concatenate([logical[:, 0], suffix_keys], axis=0)
        all_values = jnp.concatenate([logical[:, 1], suffix_values], axis=0)

        def head_attend(item):
            head_queries, head_keys, head_values = item
            scores = jnp.einsum('qrd,kd->qrk', head_queries.astype(jnp.float32), head_keys.astype(jnp.float32)) * HD ** (-0.5)
            scores = jnp.where(visible[:, None, :], scores, -jnp.inf)
            highest = lax.optimization_barrier(jnp.max(scores, axis=-1, keepdims=True))
            weights = jnp.exp(scores - highest)
            total = lax.optimization_barrier(jnp.sum(weights, axis=-1, keepdims=True))
            rounded = settle(weights).astype(jnp.float32)
            return jnp.einsum('qrk,kd->qrd', rounded, head_values.astype(jnp.float32)) / total
        result = lax.map(head_attend, (jnp.moveaxis(group_queries, 1, 0), jnp.moveaxis(all_keys, 1, 0), jnp.moveaxis(all_values, 1, 0)))
        return jnp.moveaxis(result, 0, 1).reshape(TOK_G, H * HD).astype(jnp.bfloat16)
    attn = lax.map(group_attend, jnp.arange(N_GRP, dtype=jnp.int32)).reshape(TOTAL, H * HD)
    heads_dev = H // N_TP

    def add_part(running, shard):
        offset = (shard * heads_dev * HD).astype(jnp.int32)
        columns = lax.dynamic_slice_in_dim(attn, offset, heads_dev * HD, 1)
        weight_rows = lax.dynamic_slice_in_dim(w_out, offset, heads_dev * HD, 0)
        term = settle(jnp.dot(columns, weight_rows, preferred_element_type=jnp.float32)).astype(jnp.float32)
        return (running + term, None)
    running, unused = lax.scan(add_part, jnp.zeros((TOTAL, D), jnp.float32), jnp.arange(N_TP, dtype=jnp.int32))
    return running.astype(jnp.bfloat16)
```

```python
import math

import jax
import jax.numpy as jnp
from jax import lax
from jax.experimental import pallas as pl
from jax.experimental.pallas import tpu as pltpu
from jax.sharding import PartitionSpec as P

MESH = pl.DeviceIdType.MESH
HD = 128
SINKS = 4
D = 4096
CH = 64
NZ = 8
HALF = CH * NZ
PREFIX = 4096
SCALE = HD**-0.5 * math.log2(math.e)
NEG = -1e30
BF = jnp.bfloat16
F32 = jnp.float32

RING, PZ, PY, PX, PSIB, WY, WSIB, KVZ, KVH, RS = 0, 16, 17, 20, 23, 24, 27, 30, 38, 40
MESSAGES = 56


def ring_id(base, d, h, p):
    return base + (d * 4 + (h - 1)) * 2 + p


def kernel(
    x_ref,
    gain_ref,
    pre_ref,
    kpe_ref,
    off_ref,
    cos_ref,
    sin_ref,
    wq_ref,
    wkv_ref,
    wo_ref,
    out_ref,
    xall,
    wq,
    wkv,
    wo,
    px,
    kvs,
    qpad,
    st_m,
    st_l,
    st_acc,
    attn,
    sbuf,
    rbuf,
    ssem,
    rsem,
    lsem,
):
    g = lax.axis_index("grp")
    t = lax.axis_index("tp")
    core = g % 2
    xx = (g // 2) % 4
    hi = g // 8
    z = t % NZ
    lo = t // NZ
    par = z % 2
    up = (g, lo * NZ + (z + 1) % NZ)
    down = (g, lo * NZ + (z + NZ - 1) % NZ)
    pair = (g, t + 1 - 2 * par)
    other_t = (1 - lo) * NZ + z
    other_g = (1 - hi) * 8 + xx * 2 + core
    sibling = (g + 1 - 2 * core, t)
    weight_peer = (core * other_g + (1 - core) * g, other_t)

    def along_x(k):
        return (hi * 8 + ((xx + k) % 4) * 2 + core, t)

    def half_group(k):
        index = (2 * g + lo + k + 32) % 32
        return (index // 2, (index % 2) * NZ + z)

    def remote(src, dst, number, device):
        return pltpu.make_async_remote_copy(
            src_ref=src,
            dst_ref=dst,
            send_sem=ssem.at[number],
            recv_sem=rsem.at[number],
            device_id=device,
            device_id_type=MESH,
        )

    def arrived(ref, number):
        remote(ref, ref, number, sibling).wait_recv()

    def left(ref, number):
        remote(ref, ref, number, sibling).wait_send()

    ahead = (up, down)
    sign = (1, -1)

    def rows_of(p):
        return pl.ds(p * 32, 32)

    def origin(d, h):
        return (z - sign[d] * h + NZ) % NZ

    local_wq = pltpu.make_async_copy(wq_ref, wq.at[lo], lsem.at[0])
    local_wkv = pltpu.make_async_copy(wkv_ref, wkv.at[lo], lsem.at[1])
    local_wo = pltpu.make_async_copy(wo_ref, wo.at[lo], lsem.at[2])
    local_wq.start()
    local_wkv.start()
    local_wo.start()
    wide = x_ref[...].astype(F32)
    variance = jnp.mean(wide * wide, axis=-1, keepdims=True) + 1e-05
    xall[z] = (wide * lax.rsqrt(variance) * gain_ref[...]).astype(BF)
    px[lo, hi, xx, core, par] = pre_ref[...]
    for d in range(2):
        rbuf[d, 3, rows_of(1 - d)] = jnp.zeros((32, D), BF)

    partners = [up, down, (g, other_t), (other_g, other_t), (other_g, t)]
    partners += [along_x(1), along_x(2), along_x(3), sibling]
    partners += [half_group(1), half_group(-1), half_group(2), half_group(-2)]
    barrier = pltpu.get_barrier_semaphore()
    for device in partners:
        pl.semaphore_signal(barrier, inc=1, device_id=device, device_id_type=MESH)
    pl.semaphore_wait(barrier, len(partners))

    mine = px.at[lo, hi, xx, core, par]
    remote(mine, mine, PZ, pair).start()

    def ring_send(d, h, p):
        block = xall.at[origin(d, h - 1), rows_of(p)]
        remote(block, block, ring_id(RING, d, h, p), ahead[d]).start()

    def ring_wait(d, h, p):
        arrived(xall.at[origin(d, h), rows_of(p)], ring_id(RING, d, h, p))

    for p in range(2):
        for d in range(2):
            ring_send(d, 1, p)

    def wq_half(which):
        return wq.at[which, pl.ds(pl.multiple_of(core * (D // 2), D // 2), D // 2)]

    def wkv_half(which):
        return wkv.at[which, pl.ds(pl.multiple_of(core * (D // 2), D // 2), D // 2)]

    def wo_half(which):
        return wo.at[which, pl.ds(pl.multiple_of(core * 128, 128), 128)]

    def sib_rows(ref, size):
        return ref.at[1 - lo, pl.ds(pl.multiple_of((1 - core) * size, size), size)]

    local_wq.wait()
    local_wkv.wait()
    remote(wq_half(lo), wq_half(lo), WY, weight_peer).start()
    remote(wkv_half(lo), wkv_half(lo), WY + 1, weight_peer).start()

    arrived(px.at[lo, hi, xx, core, 1 - par], PZ)
    both = px.at[lo, hi, xx, core]
    remote(both, both, PY, (g, other_t)).start()
    remote(both, both, PY + 1, (other_g, other_t)).start()
    remote(both, both, PY + 2, (other_g, t)).start()

    def ring_step(h):
        for p in range(2):
            for d in range(2):
                if h < 3 or p == d:
                    ring_wait(d, h, p)
                    ring_send(d, h + 1, p)
        if h == 3:
            for d in range(2):
                ring_wait(d, h, 1 - d)

    lane = lax.broadcasted_iota(jnp.int32, (CH, HD), 1)
    low = lane < HD // 2

    def project(c):
        rows = xall[c]
        cosine = cos_ref[c]
        sine = sin_ref[c]
        for y in range(2):
            q_part = jnp.dot(rows, wq[y], preferred_element_type=F32)
            for head in range(2):
                v = q_part[:, head * HD : (head + 1) * HD]
                turned = v * cosine + pltpu.roll(v, HD // 2, 1) * sine
                swapped = pltpu.roll(turned, HD // 2, 1)
                first = jnp.where(low, turned, 0.0)
                second = jnp.where(low, swapped, 0.0)
                qpad[y, c, pl.ds(head * CH, CH), :] = jnp.concatenate([first, second], axis=1).astype(BF)
            kv_part = jnp.dot(rows, wkv[y], preferred_element_type=F32)
            kvs[2, y, par, pl.ds(pl.multiple_of(c * CH, CH), CH)] = kv_part.astype(BF)
        block = kv_rows(par, c)
        remote(block, block, KVZ + c, pair).start()

    def kv_rows(which, c):
        return kvs.at[2, :, which, pl.ds(pl.multiple_of(c * CH, CH), CH)]

    def project_range(first, last):
        def body(k, carry):
            project((z + ((k + 1) // 2) * (2 * (k % 2) - 1) + NZ) % NZ)
            return carry

        lax.fori_loop(first, last, body, 0)

    ring_step(1)
    arrived(px.at[1 - lo, hi, xx, core], PY)
    arrived(px.at[1 - lo, 1 - hi, xx, core], PY + 1)
    arrived(px.at[lo, 1 - hi, xx, core], PY + 2)
    here = px.at[:, :, xx, core]
    for k in range(1, 4):
        remote(here, here, PX + k - 1, along_x(k)).start()
    arrived(wq_half(1 - lo), WY)
    remote(wq_half(1 - lo), wq_half(1 - lo), WSIB, sibling).start()
    arrived(wkv_half(1 - lo), WY + 1)
    remote(wkv_half(1 - lo), wkv_half(1 - lo), WSIB + 1, sibling).start()
    local_wo.wait()
    remote(wo_half(lo), wo_half(lo), WY + 2, weight_peer).start()
    ring_step(2)
    arrived(sib_rows(wq, D // 2), WSIB)
    arrived(sib_rows(wkv, D // 2), WSIB + 1)
    project_range(0, 3)
    ring_step(3)
    for k in range(1, 4):
        arrived(px.at[:, :, (xx + 4 - k) % 4, core], PX + k - 1)
    column = px.at[:, :, :, core]
    remote(column, column, PSIB, sibling).start()
    arrived(wo_half(1 - lo), WY + 2)
    remote(wo_half(1 - lo), wo_half(1 - lo), WSIB + 2, sibling).start()
    project_range(3, 7)
    ring_wait(0, 4, 0)
    ring_wait(1, 4, 1)
    project_range(7, 8)

    def kv_settle(c, carry):
        arrived(kv_rows(1 - par, c), KVZ + c)
        left(kv_rows(par, c), KVZ + c)
        rows = pl.ds(pl.multiple_of(c * CH, CH), CH)
        cosine = jnp.where(low, cos_ref[c], 1.0)
        sine = jnp.where(low, -sin_ref[c], 0.0)
        for y in range(2):
            first = kvs[2, y, 0, rows].astype(F32)
            second = kvs[2, y, 1, rows].astype(F32)
            kvs[2, y, 0, rows] = (first * cosine - second * sine).astype(BF)
            kvs[2, y, 1, rows] = (second * cosine + first * sine).astype(BF)
        return carry

    lax.fori_loop(0, NZ, kv_settle, 0)
    for k in (1, 2):
        remote(kvs.at[2], kvs.at[2 - k], KVH + k - 1, half_group(k)).start()

    def scores_of(queries, keys):
        return lax.dot_general(queries, keys, (((1,), (1,)), ((), ())), preferred_element_type=F32)

    def fold(state, queries, keys, visible):
        scores = jnp.where(visible, scores_of(queries, keys), NEG)
        highest = jnp.max(scores, axis=-1, keepdims=True)
        if state is None:
            top = highest
        else:
            top = jnp.maximum(state[0], highest)
        weights = jnp.exp2((scores - top) * SCALE)
        total = jnp.sum(weights, axis=-1, keepdims=True)
        acc = jnp.dot(weights.astype(BF), keys, preferred_element_type=F32)
        if state is None:
            return (top, total, acc)
        factor = jnp.exp2((state[0] - top) * SCALE)
        return (top, state[1] * factor + total, state[2] * factor + acc)

    def offsets(c):
        one = off_ref[c]
        return jnp.concatenate([one, one], axis=0)

    def prefix_part(c):
        offset = offsets(c)
        for y in range(2):
            queries = qpad[y, c]
            state = None
            for b in range(4):
                parts = []
                for k in range(4):
                    at = (y, b // 2, (b % 2) * 2 + k // 2, k % 2)
                    parts.append(jnp.concatenate([px[at + (0,)], px[at + (1,)]], axis=1))
                keys = jnp.concatenate(parts, axis=0)
                state = fold(state, queries, keys, kpe_ref[b] > offset)
            st_m[c, y] = state[0]
            st_l[c, y] = state[1]
            st_acc[c, y] = state[2]

    def suffix_part(c):
        offset = offsets(c)
        row = lax.broadcasted_iota(jnp.int32, (2 * CH, 1), 0) % CH + c * CH
        row = row.astype(F32)
        column_index = lax.broadcasted_iota(jnp.int32, (1, HALF), 1).astype(F32)
        for y in range(2):
            queries = qpad[y, c]
            state = (st_m[c, y], st_l[c, y], st_acc[c, y])
            for slot in range(3):
                keys = jnp.concatenate([kvs[slot, y, 0], kvs[slot, y, 1]], axis=1)
                index = column_index + (slot - 2) * HALF
                visible = (index >= row - offset) & (index <= row)
                state = fold(state, queries, keys, visible)
            result = state[2] / state[1]
            first = pltpu.roll(result[:, :HD], HD // 2, 1)
            lane2 = lax.broadcasted_iota(jnp.int32, (2 * CH, HD), 1)
            merged = jnp.where(lane2 < HD // 2, first, result[:, HD:]).astype(BF)
            attn[:, pl.ds(y * 256, HD)] = merged[:CH]
            attn[:, pl.ds(y * 256 + HD, HD)] = merged[CH:]

    tile = 1024

    def out_tile(n):
        cols = pl.ds(pl.multiple_of(n * tile, tile), tile)
        rows = attn[...]
        term = jnp.dot(rows[:, :256], wo[0, :, cols], preferred_element_type=F32)
        return cols, term + jnp.dot(rows[:, 256:], wo[1, :, cols], preferred_element_type=F32)

    def chunk_of(i):
        h = (8 - i) // 2
        return (z + h * (2 * (i % 2) - 1) + NZ) % NZ

    arrived(px.at[:, :, :, 1 - core], PSIB)

    def early(i, carry):
        prefix_part(chunk_of(i))
        return carry

    lax.fori_loop(0, 3, early, 0)
    for k in (1, 2):
        arrived(kvs.at[2 - k], KVH + k - 1)
    arrived(sib_rows(wo, 128), WSIB + 2)

    def rs_send(d, h, p):
        to = (g, lo * NZ + (z + 1 - 2 * d + NZ) % NZ)
        src = sbuf.at[d, h - 1, rows_of(p)]
        dst = rbuf.at[d, h - 1, rows_of(p)]
        remote(src, dst, ring_id(RS, d, h, p), to).start()

    def rs_wait(d, h, p):
        arrived(rbuf.at[d, h - 1, rows_of(p)], ring_id(RS, d, h, p))

    def reduce_step(i, carry):
        h = (8 - i) // 2
        d = (i + 1) % 2
        c = chunk_of(i)

        @pl.when(i >= 3)
        def _():
            prefix_part(c)

        suffix_part(c)

        @pl.when(i == 0)
        def _():
            @pl.loop(0, D // tile)
            def _(n):
                cols, term = out_tile(n)
                sbuf[0, 3, rows_of(0), cols] = term[:32].astype(BF)
                sbuf[1, 3, rows_of(1), cols] = term[32:].astype(BF)

            rs_send(0, 4, 0)
            rs_send(1, 4, 1)

        @pl.when((i > 0) & (i < 3))
        def _():
            rs_wait(d, 4, d)

        @pl.when(i >= 3)
        def _():
            @pl.when(i < 7)
            def _():
                for p in range(2):
                    rs_wait(d, h + 1, p)

        @pl.when((i > 0) & (i < 7))
        def _():
            @pl.loop(0, D // tile)
            def _(n):
                cols, term = out_tile(n)
                sbuf[d, h - 1, :, cols] = (term + rbuf[d, h, :, cols].astype(F32)).astype(BF)

            for p in range(2):
                rs_send(d, h, p)

        @pl.when(i == 7)
        def _():
            for dd in range(2):
                for p in range(2):
                    rs_wait(dd, 1, p)

            @pl.loop(0, D // tile)
            def _(n):
                cols, term = out_tile(n)
                term = term + rbuf[0, 0, :, cols].astype(F32) + rbuf[1, 0, :, cols].astype(F32)
                out_ref[:, cols] = term.astype(BF)

        return carry

    lax.fori_loop(0, 8, reduce_step, 0)

    left(mine, PZ)
    for k in range(3):
        left(both, PY + k)
        left(here, PX + k)
    left(column, PSIB)
    for k, half in enumerate((wq_half, wkv_half, wo_half)):
        left(half(lo), WY + k)
        left(half(1 - lo), WSIB + k)
    for k in range(2):
        left(kvs.at[2], KVH + k)
    for d in range(2):
        for h in range(1, 5):
            for p in range(2):
                if h < 4 or p == d:
                    left(xall.at[0, rows_of(p)], ring_id(RING, d, h, p))
                    left(sbuf.at[d, h - 1, rows_of(p)], ring_id(RS, d, h, p))


def local(x_rows, norm_gain, w_query, w_keyval, w_out, prefix_cache, page_table, request_ids):
    half_start = lax.axis_index("grp") * (2 * HALF) + (lax.axis_index("tp") // NZ) * HALF
    padded = jnp.concatenate([jnp.full((2 * HALF,), -1, jnp.int32), request_ids])
    window = lax.dynamic_slice_in_dim(padded, half_start, 3 * HALF, 0)
    own = lax.dynamic_slice_in_dim(request_ids, half_start, HALF, 0)
    earlier = jnp.arange(3 * HALF)[None, :] < jnp.arange(HALF)[:, None] + 2 * HALF
    offset = jnp.sum(((window[None, :] == own[:, None]) & earlier).astype(jnp.int32), axis=1)
    freqs = 500000.0 ** (-jnp.arange(HD // 2, dtype=F32) * 2.0 / HD)
    angles = (PREFIX + offset).astype(F32)[:, None] * freqs[None, :]
    cosine = jnp.cos(angles)
    sine = jnp.sin(angles)
    cos2 = jnp.concatenate([cosine, cosine], axis=1).reshape(NZ, CH, HD)
    sin2 = jnp.concatenate([-sine, sine], axis=1).reshape(NZ, CH, HD)
    pages = page_table.shape[0]
    labels = jnp.arange(pages, dtype=jnp.int32)
    logical = jnp.sum(jnp.where(page_table[None, :] == labels[:, None], labels[None, :], 0), axis=1)
    key_pos = logical[:, None] * HD + jnp.arange(HD, dtype=jnp.int32)[None, :]
    key_pos = jnp.where(key_pos < SINKS, 1 << 20, key_pos).astype(F32).reshape(4, 1, 1024)

    vmem = pl.BlockSpec(memory_space=pltpu.VMEM)
    hbm = pl.BlockSpec(memory_space=pl.ANY)
    return pl.pallas_call(
        kernel,
        out_shape=jax.ShapeDtypeStruct((CH, D), BF),
        in_specs=[vmem] * 7 + [hbm] * 3,
        out_specs=vmem,
        scratch_shapes=[
            pltpu.VMEM((NZ, CH, D), BF),
            pltpu.VMEM((2, D, 256), BF),
            pltpu.VMEM((2, D, 128), BF),
            pltpu.VMEM((2, 256, D), BF),
            pltpu.VMEM((2, 2, 4, 2, 2, 256, 128), BF),
            pltpu.VMEM((3, 2, 2, HALF, 128), BF),
            pltpu.VMEM((2, NZ, 2 * CH, 256), BF),
            pltpu.VMEM((NZ, 2, 2 * CH, 1), F32),
            pltpu.VMEM((NZ, 2, 2 * CH, 1), F32),
            pltpu.VMEM((NZ, 2, 2 * CH, 256), F32),
            pltpu.VMEM((CH, 512), BF),
            pltpu.VMEM((2, 4, CH, D), BF),
            pltpu.VMEM((2, 4, CH, D), BF),
            pltpu.SemaphoreType.DMA((MESSAGES,)),
            pltpu.SemaphoreType.DMA((MESSAGES,)),
            pltpu.SemaphoreType.DMA((3,)),
        ],
        compiler_params=pltpu.CompilerParams(
            collective_id=0, has_side_effects=True, vmem_limit_bytes=60 << 20
        ),
    )(
        x_rows,
        norm_gain.reshape(1, D),
        prefix_cache.reshape(256, 128),
        key_pos,
        offset.astype(F32).reshape(NZ, CH, 1),
        cos2,
        sin2,
        w_query,
        w_keyval.reshape(D, 128),
        w_out,
    )


def solution(mesh):
    placed = (
        P(("grp", "tp"), None),
        P(),
        P(None, "tp"),
        P(None, None, "tp"),
        P("tp", None),
        P("grp", None, None, "tp"),
        P(),
        P(),
    )
    return jax.shard_map(
        local, mesh=mesh, in_specs=placed, out_specs=P(("grp", "tp"), None), check_vma=False
    )
```

```python
import math

import jax
import jax.numpy as jnp
import numpy as np
from jax import lax
from jax.experimental import pallas as pl
from jax.experimental.pallas import tpu as pltpu
from jax.sharding import PartitionSpec as P

MESH = pl.DeviceIdType.MESH
HD = 128
SINKS = 4
D = 4096
CH = 64
NZ = 8
HALF = CH * NZ
PREFIX = 4096
SCALE = HD**-0.5 * math.log2(math.e)
NEG = -1e30
BF = jnp.bfloat16
F32 = jnp.float32

RING, PZ, PY, PX, PSIB, WY, WSIB, KVZ, KVH, RS = 0, 16, 17, 20, 23, 24, 27, 30, 38, 54
MESSAGES = 70


def ring_id(base, d, h, p):
    return base + (d * 4 + (h - 1)) * 2 + p


def kernel(
    x_ref,
    gain_ref,
    pre_ref,
    ids_ref,
    freq_ref,
    pages_ref,
    wq_ref,
    wkv_ref,
    wo_ref,
    out_ref,
    xall,
    wq,
    wkv,
    wo,
    px,
    kvs,
    qpad,
    st_m,
    st_l,
    st_acc,
    attn,
    kpe,
    off,
    cosines,
    sines,
    tbuf,
    sbuf,
    rbuf,
    ssem,
    rsem,
    lsem,
):
    g = lax.axis_index("grp")
    t = lax.axis_index("tp")
    core = g % 2
    xx = (g // 2) % 4
    hi = g // 8
    z = t % NZ
    lo = t // NZ
    par = z % 2
    up = (g, lo * NZ + (z + 1) % NZ)
    down = (g, lo * NZ + (z + NZ - 1) % NZ)
    pair = (g, t + 1 - 2 * par)
    other_t = (1 - lo) * NZ + z
    other_g = (1 - hi) * 8 + xx * 2 + core
    sibling = (g + 1 - 2 * core, t)
    weight_peer = (core * other_g + (1 - core) * g, other_t)

    def along_x(k):
        return (hi * 8 + ((xx + k) % 4) * 2 + core, t)

    def half_group(k):
        index = (2 * g + lo + k + 32) % 32
        return (index // 2, (index % 2) * NZ + z)

    def remote(src, dst, number, device):
        return pltpu.make_async_remote_copy(
            src_ref=src,
            dst_ref=dst,
            send_sem=ssem.at[number],
            recv_sem=rsem.at[number],
            device_id=device,
            device_id_type=MESH,
        )

    def arrived(ref, number):
        remote(ref, ref, number, sibling).wait_recv()

    def left(ref, number):
        remote(ref, ref, number, sibling).wait_send()

    ahead = (up, down)
    sign = (1, -1)

    def rows_of(p):
        return pl.ds(p * 32, 32)

    def origin(d, h):
        return (z - sign[d] * h + NZ) % NZ

    local_wq = pltpu.make_async_copy(wq_ref, wq.at[lo], lsem.at[0])
    local_wkv = pltpu.make_async_copy(wkv_ref, wkv.at[lo], lsem.at[1])
    local_wo = pltpu.make_async_copy(wo_ref, wo.at[lo], lsem.at[2])
    local_wq.start()
    local_wkv.start()
    local_wo.start()
    wide = x_ref[...].astype(F32)
    variance = jnp.mean(wide * wide, axis=-1, keepdims=True) + 1e-05
    xall[z] = (wide * lax.rsqrt(variance) * gain_ref[...]).astype(BF)
    for page in range(2):
        rows = pl.ds(page * 128, 128)
        px[lo, hi, xx, core, par, rows, :] = pre_ref[rows, :].astype(F32).T.astype(BF)
    for d in range(2):
        rbuf[d, 3, rows_of(1 - d)] = jnp.zeros((32, D), BF)

    partners = [up, down, (g, other_t), (other_g, other_t), (other_g, t)]
    partners += [along_x(1), along_x(2), along_x(3), sibling]
    partners += [half_group(1), half_group(-1), half_group(2), half_group(-2)]
    barrier = pltpu.get_barrier_semaphore()
    for device in partners:
        pl.semaphore_signal(barrier, inc=1, device_id=device, device_id_type=MESH)
    pl.semaphore_wait(barrier, len(partners))

    mine = px.at[lo, hi, xx, core, par]
    remote(mine, mine, PZ, pair).start()

    def ring_send(d, h, p):
        block = xall.at[origin(d, h - 1), rows_of(p)]
        remote(block, block, ring_id(RING, d, h, p), ahead[d]).start()

    def ring_wait(d, h, p):
        arrived(xall.at[origin(d, h), rows_of(p)], ring_id(RING, d, h, p))

    for p in range(2):
        for d in range(2):
            ring_send(d, 1, p)

    def wq_half(which):
        return wq.at[which, pl.ds(pl.multiple_of(core * (D // 2), D // 2), D // 2)]

    def wkv_half(which):
        return wkv.at[which, pl.ds(pl.multiple_of(core * 64, 64), 64)]

    def wo_half(which):
        return wo.at[which, pl.ds(pl.multiple_of(core * 128, 128), 128)]

    def sib_rows(ref, size):
        return ref.at[1 - lo, pl.ds(pl.multiple_of((1 - core) * size, size), size)]

    local_wq.wait()
    local_wkv.wait()
    remote(wq_half(lo), wq_half(lo), WY, weight_peer).start()
    remote(wkv_half(lo), wkv_half(lo), WY + 1, weight_peer).start()

    arrived(px.at[lo, hi, xx, core, 1 - par], PZ)
    both = px.at[lo, hi, xx, core]
    remote(both, both, PY, (g, other_t)).start()
    remote(both, both, PY + 1, (other_g, other_t)).start()
    remote(both, both, PY + 2, (other_g, t)).start()

    def ring_step(h):
        for p in range(2):
            for d in range(2):
                if h < 3 or p == d:
                    ring_wait(d, h, p)
                    ring_send(d, h + 1, p)
        if h == 3:
            for d in range(2):
                ring_wait(d, h, 1 - d)

    lane = lax.broadcasted_iota(jnp.int32, (CH, HD), 1)
    low = lane < HD // 2

    def project(c, y):
        rows = xall[c]
        cosine = cosines[c]
        sine = sines[c]
        q_part = jnp.dot(rows, wq[y], preferred_element_type=F32)
        for head in range(2):
            v = q_part[:, head * HD : (head + 1) * HD]
            turned = v * cosine + pltpu.roll(v, HD // 2, 1) * sine
            swapped = pltpu.roll(turned, HD // 2, 1)
            first = jnp.where(low, turned, 0.0)
            second = jnp.where(low, swapped, 0.0)
            qpad[y, c, pl.ds(head * CH, CH), :] = jnp.concatenate([first, second], axis=1).astype(BF)
        kv_part = scores_of(rows, wkv[y])
        kvs[2, y, par, pl.ds(pl.multiple_of(c * CH, CH), CH)] = kv_part.astype(BF)

    def scores_of(queries, keys):
        return lax.dot_general(queries, keys, (((1,), (1,)), ((), ())), preferred_element_type=F32)

    def kv_rows(which, c):
        return kvs.at[2, :, which, pl.ds(pl.multiple_of(c * CH, CH), CH)]

    def in_order(k):
        return (z + ((k + 1) // 2) * (2 * (k % 2) - 1) + NZ) % NZ

    def project_own(first, last):
        def body(k, carry):
            project(in_order(k), lo)
            return carry

        lax.fori_loop(first, last, body, 0)

    def project_other(first, last):
        def body(k, carry):
            c = in_order(k)
            project(c, 1 - lo)
            block = kv_rows(par, c)
            remote(block, block, KVZ + c, pair).start()
            return carry

        lax.fori_loop(first, last, body, 0)

    pieces = []
    for k in range(3):
        block = 2 * g + lo - 2 + k
        for r in range(4):
            ids = ids_ref[pl.ds(jnp.maximum(block, 0) * 4 + r, 1), :].astype(F32)
            pieces.append(jnp.where(block >= 0, ids, -1.0))
    window = jnp.concatenate(pieces, axis=1)

    def tables(c, carry):
        row = lax.broadcasted_iota(jnp.int32, (CH, 3 * HALF), 0) + c * CH + 2 * HALF
        col = lax.broadcasted_iota(jnp.int32, (CH, 3 * HALF), 1)
        own = jnp.sum(jnp.where(col == row, window, 0.0), axis=1, keepdims=True)
        earlier = (window == own) & (col < row)
        offset = jnp.sum(jnp.where(earlier, 1.0, 0.0), axis=1, keepdims=True)
        off[c] = offset
        angles = (PREFIX + offset) * freq_ref[...]
        sine = jnp.sin(angles)
        cosines[c] = jnp.cos(angles)
        sines[c] = jnp.where(low, -sine, sine)
        return carry

    lax.fori_loop(0, NZ, tables, 0)
    page_row = lax.broadcasted_iota(jnp.int32, (32, 128), 0)
    logical = jnp.zeros((32, 128), F32)
    for page in range(32):
        logical = logical + jnp.where(page_row == pages_ref[page], float(page), 0.0)
    key_pos = logical * 128.0 + lax.broadcasted_iota(jnp.int32, (32, 128), 1).astype(F32)
    kpe[...] = jnp.where(key_pos < SINKS, 1e6, key_pos)
    project_own(0, 1)

    def kv_settle(c):
        arrived(kv_rows(1 - par, c), KVZ + c)
        left(kv_rows(par, c), KVZ + c)
        rows = pl.ds(pl.multiple_of(c * CH, CH), CH)
        cosine = jnp.where(low, cosines[c], 1.0)
        sine = jnp.where(low, -sines[c], 0.0)
        for y in range(2):
            first = kvs[2, y, 0, rows].astype(F32)
            second = kvs[2, y, 1, rows].astype(F32)
            kvs[2, y, 0, rows] = (first * cosine - second * sine).astype(BF)
            kvs[2, y, 1, rows] = (second * cosine + first * sine).astype(BF)
        for k in (1, 2):
            remote(kv_chunk(2, c), kv_chunk(2 - k, c), KVH + 2 * c + k - 1, half_group(k)).start()

    def kv_chunk(slot, c):
        return kvs.at[slot, :, :, pl.ds(pl.multiple_of(c * CH, CH), CH)]

    def settle(first, last):
        def body(k, carry):
            kv_settle(in_order(k))
            return carry

        lax.fori_loop(first, last, body, 0)

    def fold(state, queries, keys, visible):
        scores = jnp.where(visible, scores_of(queries, keys), NEG)
        highest = jnp.max(scores, axis=-1, keepdims=True)
        if state is None:
            top = highest
        else:
            top = jnp.maximum(state[0], highest)
        weights = jnp.exp2((scores - top) * SCALE)
        total = jnp.sum(weights, axis=-1, keepdims=True)
        acc = jnp.dot(weights.astype(BF), keys, preferred_element_type=F32)
        if state is None:
            return (top, total, acc)
        factor = jnp.exp2((state[0] - top) * SCALE)
        return (top, state[1] * factor + total, state[2] * factor + acc)

    def offsets(c):
        one = off[c]
        return jnp.concatenate([one, one], axis=0)

    def prefix_part(c):
        offset = offsets(c)
        for y in range(2):
            queries = qpad[y, c]
            state = None
            for b in range(4):
                parts = []
                for k in range(4):
                    at = (y, b // 2, (b % 2) * 2 + k // 2, k % 2)
                    parts.append(jnp.concatenate([px[at + (0,)], px[at + (1,)]], axis=1))
                keys = jnp.concatenate(parts, axis=0)
                positions = jnp.concatenate([kpe[pl.ds(8 * b + r, 1), :] for r in range(8)], axis=1)
                state = fold(state, queries, keys, positions > offset)
            st_m[c, y] = state[0]
            st_l[c, y] = state[1]
            st_acc[c, y] = state[2]

    def suffix_part(c, slot_out):
        offset = offsets(c)
        row = lax.broadcasted_iota(jnp.int32, (2 * CH, 1), 0) % CH + c * CH
        row = row.astype(F32)
        column_index = lax.broadcasted_iota(jnp.int32, (1, HALF), 1).astype(F32)
        for y in range(2):
            queries = qpad[y, c]
            state = (st_m[c, y], st_l[c, y], st_acc[c, y])
            for slot in range(3):
                keys = jnp.concatenate([kvs[slot, y, 0], kvs[slot, y, 1]], axis=1)
                index = column_index + (slot - 2) * HALF
                visible = (index >= row - offset) & (index <= row)
                state = fold(state, queries, keys, visible)
            result = state[2] / state[1]
            first = pltpu.roll(result[:, :HD], HD // 2, 1)
            lane2 = lax.broadcasted_iota(jnp.int32, (2 * CH, HD), 1)
            merged = jnp.where(lane2 < HD // 2, first, result[:, HD:]).astype(BF)
            attn[slot_out, :, pl.ds(y * 256, HD)] = merged[:CH]
            attn[slot_out, :, pl.ds(y * 256 + HD, HD)] = merged[CH:]

    tile = 1024

    def out_terms(slot):
        @pl.loop(0, D // tile)
        def _(n):
            cols = pl.ds(pl.multiple_of(n * tile, tile), tile)
            rows = attn[slot]
            term = jnp.dot(rows[:, :256], wo[0, :, cols], preferred_element_type=F32)
            tbuf[slot, :, cols] = term + jnp.dot(rows[:, 256:], wo[1, :, cols], preferred_element_type=F32)

    def rs_send(d, h, p):
        src = sbuf.at[d, h - 1, rows_of(p)]
        dst = rbuf.at[d, h - 1, rows_of(p)]
        remote(src, dst, ring_id(RS, d, h, p), ahead[d]).start()

    def rs_wait(d, h, p):
        arrived(rbuf.at[d, h - 1, rows_of(p)], ring_id(RS, d, h, p))

    ring_step(1)
    arrived(px.at[1 - lo, hi, xx, core], PY)
    arrived(px.at[1 - lo, 1 - hi, xx, core], PY + 1)
    arrived(px.at[lo, 1 - hi, xx, core], PY + 2)
    here = px.at[:, :, xx, core]
    for k in range(1, 4):
        remote(here, here, PX + k - 1, along_x(k)).start()
    project_own(1, 3)
    ring_step(2)
    arrived(wq_half(1 - lo), WY)
    remote(wq_half(1 - lo), wq_half(1 - lo), WSIB, sibling).start()
    arrived(wkv_half(1 - lo), WY + 1)
    remote(wkv_half(1 - lo), wkv_half(1 - lo), WSIB + 1, sibling).start()
    local_wo.wait()
    remote(wo_half(lo), wo_half(lo), WY + 2, weight_peer).start()
    project_own(3, 5)
    arrived(sib_rows(wq, D // 2), WSIB)
    arrived(sib_rows(wkv, 64), WSIB + 1)
    project_other(0, 5)
    ring_step(3)
    for k in range(1, 4):
        arrived(px.at[:, :, (xx + 4 - k) % 4, core], PX + k - 1)
    column = px.at[:, :, :, core]
    remote(column, column, PSIB, sibling).start()
    project_own(5, 7)
    project_other(5, 7)
    settle(0, 5)
    ring_wait(0, 4, 0)
    ring_wait(1, 4, 1)
    project_own(7, 8)
    project_other(7, 8)
    arrived(wo_half(1 - lo), WY + 2)
    remote(wo_half(1 - lo), wo_half(1 - lo), WSIB + 2, sibling).start()
    arrived(px.at[:, :, :, 1 - core], PSIB)

    def early(k, carry):
        prefix_part(in_order(k))
        return carry

    lax.fori_loop(7, 8, early, 0)
    settle(5, 8)
    lax.fori_loop(5, 7, early, 0)

    def kv_arrive(c, carry):
        for k in (1, 2):
            arrived(kv_chunk(2 - k, c), KVH + 2 * c + k - 1)
        return carry

    lax.fori_loop(0, NZ, kv_arrive, 0)
    arrived(sib_rows(wo, 128), WSIB + 2)

    col_tiles = [pl.ds(n * tile, tile) for n in range(D // tile)]
    suffix_part((z + 4) % NZ, 0)
    out_terms(0)
    for d in range(2):
        for cols in col_tiles:
            sbuf[d, 3, rows_of(d), cols] = tbuf[0, rows_of(d), cols].astype(BF)
        rs_send(d, 4, d)

    def reduce_step(i, carry):
        h = 3 - i

        def terms(d, carry):
            c = (z + (1 - 2 * d) * h + NZ) % NZ

            @pl.when(i > 0)
            def _():
                prefix_part(c)

            suffix_part(c, d)
            out_terms(d)
            return carry

        lax.fori_loop(0, 2, terms, 0)
        for fresh in (True, False):
            for d in range(2):
                p = 1 - d if fresh else d
                if fresh:

                    @pl.when(i > 0)
                    def _():
                        rs_wait(d, h + 1, p)

                else:
                    rs_wait(d, h + 1, p)
                for cols in col_tiles:
                    total = tbuf[d, rows_of(p), cols] + rbuf[d, h, rows_of(p), cols].astype(F32)
                    sbuf[d, h - 1, rows_of(p), cols] = total.astype(BF)
                rs_send(d, h, p)
        return carry

    lax.fori_loop(0, 3, reduce_step, 0)
    prefix_part(z)
    suffix_part(z, 0)
    out_terms(0)
    for p in range(2):
        for d in range(2):
            rs_wait(d, 1, p)
        for cols in col_tiles:
            total = tbuf[0, rows_of(p), cols] + rbuf[0, 0, rows_of(p), cols].astype(F32)
            out_ref[rows_of(p), cols] = (total + rbuf[1, 0, rows_of(p), cols].astype(F32)).astype(BF)

    left(mine, PZ)
    for k in range(3):
        left(both, PY + k)
        left(here, PX + k)
    left(column, PSIB)
    for k, half in enumerate((wq_half, wkv_half, wo_half)):
        left(half(lo), WY + k)
        left(half(1 - lo), WSIB + k)

    def kv_left(c, carry):
        for k in (1, 2):
            left(kv_chunk(2, c), KVH + 2 * c + k - 1)
        return carry

    lax.fori_loop(0, NZ, kv_left, 0)
    for d in range(2):
        for h in range(1, 5):
            for p in range(2):
                if h < 4 or p == d:
                    left(xall.at[0, rows_of(p)], ring_id(RING, d, h, p))
                    left(sbuf.at[d, h - 1, rows_of(p)], ring_id(RS, d, h, p))


def local(x_rows, norm_gain, w_query, w_keyval, w_out, prefix_cache, page_table, request_ids):
    exponents = -(np.arange(HD) % (HD // 2)) * 2.0 / HD
    freqs = jnp.asarray((500000.0**exponents).astype(np.float32)).reshape(1, HD)
    vmem = pl.BlockSpec(memory_space=pltpu.VMEM)
    hbm = pl.BlockSpec(memory_space=pl.ANY)
    return pl.pallas_call(
        kernel,
        out_shape=jax.ShapeDtypeStruct((CH, D), BF),
        in_specs=[vmem] * 5 + [pl.BlockSpec(memory_space=pltpu.SMEM)] + [hbm] * 3,
        out_specs=vmem,
        scratch_shapes=[
            pltpu.VMEM((NZ, CH, D), BF),
            pltpu.VMEM((2, D, 256), BF),
            pltpu.VMEM((2, 128, D), BF),
            pltpu.VMEM((2, 256, D), BF),
            pltpu.VMEM((2, 2, 4, 2, 2, 256, 128), BF),
            pltpu.VMEM((3, 2, 2, HALF, 128), BF),
            pltpu.VMEM((2, NZ, 2 * CH, 256), BF),
            pltpu.VMEM((NZ, 2, 2 * CH, 1), F32),
            pltpu.VMEM((NZ, 2, 2 * CH, 1), F32),
            pltpu.VMEM((NZ, 2, 2 * CH, 256), F32),
            pltpu.VMEM((2, CH, 512), BF),
            pltpu.VMEM((32, 128), F32),
            pltpu.VMEM((NZ, CH, 1), F32),
            pltpu.VMEM((NZ, CH, HD), F32),
            pltpu.VMEM((NZ, CH, HD), F32),
            pltpu.VMEM((2, CH, D), F32),
            pltpu.VMEM((2, 4, CH, D), BF),
            pltpu.VMEM((2, 4, CH, D), BF),
            pltpu.SemaphoreType.DMA((MESSAGES,)),
            pltpu.SemaphoreType.DMA((MESSAGES,)),
            pltpu.SemaphoreType.DMA((3,)),
        ],
        compiler_params=pltpu.CompilerParams(
            collective_id=0, has_side_effects=True, vmem_limit_bytes=60 << 20
        ),
    )(
        x_rows,
        norm_gain.reshape(1, D),
        prefix_cache.transpose(0, 2, 3, 1).reshape(256, 128),
        request_ids.reshape(128, 128),
        freqs,
        page_table,
        w_query,
        w_keyval.transpose(1, 2, 0).reshape(128, D),
        w_out,
    )


def solution(mesh):
    placed = (
        P(("grp", "tp"), None),
        P(),
        P(None, "tp"),
        P(None, None, "tp"),
        P("tp", None),
        P("grp", None, None, "tp"),
        P(),
        P(),
    )
    return jax.shard_map(
        local, mesh=mesh, in_specs=placed, out_specs=P(("grp", "tp"), None), check_vma=False
    )
```

```python
import math

import jax
import jax.numpy as jnp
import numpy as np
from jax import lax
from jax.experimental import pallas as pl
from jax.experimental.pallas import tpu as pltpu
from jax.sharding import PartitionSpec as P

MESH = pl.DeviceIdType.MESH
HD = 128
SINKS = 4
D = 4096
CH = 64
NZ = 8
HALF = CH * NZ
PREFIX = 4096
SCALE = HD**-0.5 * math.log2(math.e)
NEG = -1e30
BF = jnp.bfloat16
F32 = jnp.float32

RING, PZ, PY, PX, PSIB, WY, WSIB, KVZ, KVH, RS = 0, 16, 17, 20, 24, 25, 28, 31, 39, 55
MESSAGES = 71


def ring_id(base, d, h, p):
    return base + (d * 4 + (h - 1)) * 2 + p


def kernel(
    x_ref,
    gain_ref,
    pre_ref,
    ids_ref,
    freq_ref,
    pages_ref,
    wq_ref,
    wkv_ref,
    wo_ref,
    out_ref,
    xall,
    wq,
    wkv,
    wo,
    px,
    kvs,
    qpad,
    st_m,
    st_l,
    st_acc,
    attn,
    kpe,
    off,
    cosines,
    sines,
    tbuf,
    sbuf,
    rbuf,
    ssem,
    rsem,
    lsem,
):
    g = lax.axis_index("grp")
    t = lax.axis_index("tp")
    core = g % 2
    xx = (g // 2) % 4
    hi = g // 8
    z = t % NZ
    lo = t // NZ
    par = z % 2
    up = (g, lo * NZ + (z + 1) % NZ)
    down = (g, lo * NZ + (z + NZ - 1) % NZ)
    pair = (g, t + 1 - 2 * par)
    other_t = (1 - lo) * NZ + z
    other_g = (1 - hi) * 8 + xx * 2 + core
    sibling = (g + 1 - 2 * core, t)
    weight_peer = (core * other_g + (1 - core) * g, other_t)

    def along_x(k):
        return (hi * 8 + ((xx + k) % 4) * 2 + core, t)

    def half_group(k):
        index = (2 * g + lo + k + 32) % 32
        return (index // 2, (index % 2) * NZ + z)

    def remote(src, dst, number, device):
        return pltpu.make_async_remote_copy(
            src_ref=src,
            dst_ref=dst,
            send_sem=ssem.at[number],
            recv_sem=rsem.at[number],
            device_id=device,
            device_id_type=MESH,
        )

    def arrived(ref, number):
        remote(ref, ref, number, sibling).wait_recv()

    def left(ref, number):
        remote(ref, ref, number, sibling).wait_send()

    ahead = (up, down)
    sign = (1, -1)

    def rows_of(p):
        return pl.ds(p * 32, 32)

    def origin(d, h):
        return (z - sign[d] * h + NZ) % NZ

    local_wq = pltpu.make_async_copy(wq_ref, wq.at[lo], lsem.at[0])
    local_wkv = pltpu.make_async_copy(wkv_ref, wkv.at[lo], lsem.at[1])
    local_wo = pltpu.make_async_copy(wo_ref, wo.at[lo], lsem.at[2])
    local_wq.start()
    local_wkv.start()
    local_wo.start()
    wide = x_ref[...].astype(F32)
    variance = jnp.mean(wide * wide, axis=-1, keepdims=True) + 1e-05
    xall[z] = (wide * lax.rsqrt(variance) * gain_ref[...]).astype(BF)
    for page in range(2):
        rows = pl.ds(page * 128, 128)
        px[lo, hi, xx, core, par, rows, :] = pre_ref[rows, :].astype(F32).T.astype(BF)
    for d in range(2):
        rbuf[d, 3, rows_of(1 - d)] = jnp.zeros((32, D), BF)

    partners = [up, down, (g, other_t), (other_g, other_t), (other_g, t)]
    partners += [along_x(1), along_x(3), sibling]
    partners += [half_group(1), half_group(-1), half_group(2), half_group(-2)]
    barrier = pltpu.get_barrier_semaphore()
    for device in partners:
        pl.semaphore_signal(barrier, inc=1, device_id=device, device_id_type=MESH)
    pl.semaphore_wait(barrier, len(partners))

    mine = px.at[lo, hi, xx, core, par]
    remote(mine, mine, PZ, pair).start()

    def ring_send(d, h, p):
        block = xall.at[origin(d, h - 1), rows_of(p)]
        remote(block, block, ring_id(RING, d, h, p), ahead[d]).start()

    def ring_wait(d, h, p):
        arrived(xall.at[origin(d, h), rows_of(p)], ring_id(RING, d, h, p))

    for p in range(2):
        for d in range(2):
            ring_send(d, 1, p)

    def wq_half(which):
        return wq.at[which, pl.ds(pl.multiple_of(core * (D // 2), D // 2), D // 2)]

    def wkv_half(which):
        return wkv.at[which, pl.ds(pl.multiple_of(core * 64, 64), 64)]

    def wo_half(which):
        return wo.at[which, pl.ds(pl.multiple_of(core * 128, 128), 128)]

    def sib_rows(ref, size):
        return ref.at[1 - lo, pl.ds(pl.multiple_of((1 - core) * size, size), size)]

    arrived(px.at[lo, hi, xx, core, 1 - par], PZ)
    both = px.at[lo, hi, xx, core]
    remote(both, both, PY, (g, other_t)).start()
    remote(both, both, PY + 1, (other_g, other_t)).start()
    remote(both, both, PY + 2, (other_g, t)).start()

    def ring_step(h):
        for p in range(2):
            for d in range(2):
                if h < 3 or p == d:
                    ring_wait(d, h, p)
                    ring_send(d, h + 1, p)
        if h == 3:
            for d in range(2):
                ring_wait(d, h, 1 - d)

    lane = lax.broadcasted_iota(jnp.int32, (CH, HD), 1)
    low = lane < HD // 2

    def project_kv(chunks, y):
        rows = jnp.concatenate([xall[c] for c in chunks], axis=0)
        kv_part = scores_of(rows, wkv[y]).astype(BF)
        for n, c in enumerate(chunks):
            kvs[2, y, par, pl.ds(pl.multiple_of(c * CH, CH), CH)] = kv_part[n * CH : (n + 1) * CH]

    def project_q(chunks, y):
        rows = jnp.concatenate([xall[c] for c in chunks], axis=0)
        q_part = jnp.dot(rows, wq[y], preferred_element_type=F32)
        for n, c in enumerate(chunks):
            cosine = cosines[c]
            sine = sines[c]
            for head in range(2):
                v = q_part[n * CH : (n + 1) * CH, head * HD : (head + 1) * HD]
                turned = v * cosine + pltpu.roll(v, HD // 2, 1) * sine
                swapped = pltpu.roll(turned, HD // 2, 1)
                first = jnp.where(low, turned, 0.0)
                second = jnp.where(low, swapped, 0.0)
                both_halves = jnp.concatenate([first, second], axis=1).astype(BF)
                qpad[y, c, pl.ds(head * CH, CH), :] = both_halves

    def scores_of(queries, keys):
        return lax.dot_general(queries, keys, (((1,), (1,)), ((), ())), preferred_element_type=F32)

    def kv_rows(which, c):
        return kvs.at[2, :, which, pl.ds(pl.multiple_of(c * CH, CH), CH)]

    def in_order(k):
        return (z + ((k + 1) // 2) * (2 * (k % 2) - 1) + NZ) % NZ

    def send_kv(chunks):
        for c in chunks:
            block = kv_rows(par, c)
            remote(block, block, KVZ + c, pair).start()

    def around(h):
        return ((z + h) % NZ, (z + NZ - h) % NZ)

    def project_pairs(first, last, y, whole):
        def body(h, carry):
            chunks = around(h)
            project_kv(chunks, y)
            if whole:
                send_kv(chunks)
            project_q(chunks, y)
            return carry

        lax.fori_loop(first, last, body, 0)

    pieces = []
    for k in range(3):
        block = 2 * g + lo - 2 + k
        for r in range(4):
            ids = ids_ref[pl.ds(jnp.maximum(block, 0) * 4 + r, 1), :].astype(F32)
            pieces.append(jnp.where(block >= 0, ids, -1.0))
    window = jnp.concatenate(pieces, axis=1)

    def tables(c, carry):
        row = lax.broadcasted_iota(jnp.int32, (CH, 3 * HALF), 0) + c * CH + 2 * HALF
        col = lax.broadcasted_iota(jnp.int32, (CH, 3 * HALF), 1)
        own = jnp.sum(jnp.where(col == row, window, 0.0), axis=1, keepdims=True)
        earlier = (window == own) & (col < row)
        offset = jnp.sum(jnp.where(earlier, 1.0, 0.0), axis=1, keepdims=True)
        off[c] = offset
        angles = (PREFIX + offset) * freq_ref[...]
        sine = jnp.sin(angles)
        cosines[c] = jnp.cos(angles)
        sines[c] = jnp.where(low, -sine, sine)
        return carry

    lax.fori_loop(0, NZ, tables, 0)
    page_row = lax.broadcasted_iota(jnp.int32, (32, 128), 0)
    logical = jnp.zeros((32, 128), F32)
    for page in range(32):
        logical = logical + jnp.where(page_row == pages_ref[page], float(page), 0.0)
    key_pos = logical * 128.0 + lax.broadcasted_iota(jnp.int32, (32, 128), 1).astype(F32)
    kpe[...] = jnp.where(key_pos < SINKS, 1e6, key_pos)
    def kv_settle(c):
        arrived(kv_rows(1 - par, c), KVZ + c)
        left(kv_rows(par, c), KVZ + c)
        rows = pl.ds(pl.multiple_of(c * CH, CH), CH)
        cosine = jnp.where(low, cosines[c], 1.0)
        sine = jnp.where(low, -sines[c], 0.0)
        for y in range(2):
            first = kvs[2, y, 0, rows].astype(F32)
            second = kvs[2, y, 1, rows].astype(F32)
            kvs[2, y, 0, rows] = (first * cosine - second * sine).astype(BF)
            kvs[2, y, 1, rows] = (second * cosine + first * sine).astype(BF)
        for k in (1, 2):
            remote(kv_chunk(2, c), kv_chunk(2 - k, c), KVH + 2 * c + k - 1, half_group(k)).start()

    def kv_chunk(slot, c):
        return kvs.at[slot, :, :, pl.ds(pl.multiple_of(c * CH, CH), CH)]

    def settle(first, last):
        def body(k, carry):
            kv_settle(in_order(k))
            return carry

        lax.fori_loop(first, last, body, 0)

    def fold(state, queries, keys, visible):
        scores = jnp.where(visible, scores_of(queries, keys), NEG)
        highest = jnp.max(scores, axis=-1, keepdims=True)
        if state is None:
            top = highest
        else:
            top = jnp.maximum(state[0], highest)
        weights = jnp.exp2((scores - top) * SCALE)
        total = jnp.sum(weights, axis=-1, keepdims=True)
        acc = jnp.dot(weights.astype(BF), keys, preferred_element_type=F32)
        if state is None:
            return (top, total, acc)
        factor = jnp.exp2((state[0] - top) * SCALE)
        return (top, state[1] * factor + total, state[2] * factor + acc)

    def pair_queries(chunks, y):
        return jnp.concatenate([qpad[y, c] for c in chunks], axis=0)

    def pair_offsets(chunks):
        return jnp.concatenate([off[c] for c in chunks for _ in range(2)], axis=0)

    def prefix_part(chunks):
        offset = pair_offsets(chunks)
        for y in range(2):
            queries = pair_queries(chunks, y)
            state = None
            for b in range(4):
                parts = []
                for k in range(4):
                    at = (y, b // 2, (b % 2) * 2 + k // 2, k % 2)
                    parts.append(jnp.concatenate([px[at + (0,)], px[at + (1,)]], axis=1))
                keys = jnp.concatenate(parts, axis=0)
                positions = jnp.concatenate([kpe[pl.ds(8 * b + r, 1), :] for r in range(8)], axis=1)
                state = fold(state, queries, keys, positions > offset)
            for n, c in enumerate(chunks):
                st_m[c, y] = state[0][n * 2 * CH : (n + 1) * 2 * CH]
                st_l[c, y] = state[1][n * 2 * CH : (n + 1) * 2 * CH]
                st_acc[c, y] = state[2][n * 2 * CH : (n + 1) * 2 * CH]

    def suffix_part(chunks):
        offset = pair_offsets(chunks)
        row = lax.broadcasted_iota(jnp.int32, (2 * CH, 1), 0) % CH
        row = jnp.concatenate([row + c * CH for c in chunks], axis=0).astype(F32)
        column_index = lax.broadcasted_iota(jnp.int32, (1, HALF), 1).astype(F32)
        lane2 = lax.broadcasted_iota(jnp.int32, (2 * CH * len(chunks), HD), 1)
        for y in range(2):
            queries = pair_queries(chunks, y)
            state = tuple(
                jnp.concatenate([ref[c, y] for c in chunks], axis=0) for ref in (st_m, st_l, st_acc)
            )
            for slot in range(3):
                keys = jnp.concatenate([kvs[slot, y, 0], kvs[slot, y, 1]], axis=1)
                index = column_index + (slot - 2) * HALF
                visible = (index >= row - offset) & (index <= row)
                state = fold(state, queries, keys, visible)
            result = state[2] / state[1]
            first = pltpu.roll(result[:, :HD], HD // 2, 1)
            merged = jnp.where(lane2 < HD // 2, first, result[:, HD:]).astype(BF)
            for n in range(len(chunks)):
                for head in range(2):
                    part = merged[(2 * n + head) * CH : (2 * n + head + 1) * CH]
                    attn[pl.ds(n * CH, CH), pl.ds(y * 256 + head * HD, HD)] = part

    tile = 1024

    def out_terms(second):
        @pl.loop(0, D // tile)
        def _(n):
            cols = pl.ds(pl.multiple_of(n * tile, tile), tile)
            rows = attn[...]
            term = jnp.dot(rows[:, :256], wo[0, :, cols], preferred_element_type=F32)
            term = term + jnp.dot(rows[:, 256:], wo[1, :, cols], preferred_element_type=F32)
            tbuf[0, :, cols] = term[:CH]
            tbuf[second, :, cols] = term[CH:]

    def rs_send(d, h, p):
        src = sbuf.at[d, h - 1, rows_of(p)]
        dst = rbuf.at[d, h - 1, rows_of(p)]
        remote(src, dst, ring_id(RS, d, h, p), ahead[d]).start()

    def rs_wait(d, h, p):
        arrived(rbuf.at[d, h - 1, rows_of(p)], ring_id(RS, d, h, p))

    arrived(px.at[1 - lo, hi, xx, core], PY)
    arrived(px.at[1 - lo, 1 - hi, xx, core], PY + 1)
    arrived(px.at[lo, 1 - hi, xx, core], PY + 2)

    def x_block(k):
        return px.at[:, :, (xx + k) % 4, core]

    def x_half(k, which):
        return px.at[:, :, (xx + k) % 4, core, which]

    remote(x_block(0), x_block(0), PX, along_x(1)).start()
    remote(x_block(0), x_block(0), PX + 1, along_x(3)).start()
    local_wq.wait()
    local_wkv.wait()
    remote(wkv_half(lo), wkv_half(lo), WY + 1, weight_peer).start()
    remote(wq_half(lo), wq_half(lo), WY, weight_peer).start()
    project_kv((z,), lo)
    project_q((z,), lo)
    ring_step(1)
    project_pairs(1, 2, lo, False)
    arrived(x_block(3), PX)
    remote(x_half(3, 0), x_half(3, 0), PX + 2, along_x(1)).start()
    arrived(x_block(1), PX + 1)
    remote(x_half(1, 1), x_half(1, 1), PX + 3, along_x(3)).start()
    ring_step(2)
    arrived(wkv_half(1 - lo), WY + 1)
    remote(wkv_half(1 - lo), wkv_half(1 - lo), WSIB + 1, sibling).start()
    arrived(wq_half(1 - lo), WY)
    remote(wq_half(1 - lo), wq_half(1 - lo), WSIB, sibling).start()
    local_wo.wait()
    remote(wo_half(lo), wo_half(lo), WY + 2, weight_peer).start()
    arrived(x_half(2, 0), PX + 2)
    arrived(x_half(2, 1), PX + 3)
    column = px.at[:, :, :, core]
    remote(column, column, PSIB, sibling).start()
    project_pairs(2, 3, lo, False)
    arrived(sib_rows(wq, D // 2), WSIB)
    arrived(sib_rows(wkv, 64), WSIB + 1)
    project_kv((z,), 1 - lo)
    send_kv((z,))
    project_q((z,), 1 - lo)
    project_pairs(1, 3, 1 - lo, True)
    ring_step(3)
    project_pairs(3, 4, lo, False)
    project_pairs(3, 4, 1 - lo, True)
    settle(0, 5)
    arrived(px.at[:, :, :, 1 - core], PSIB)
    ring_wait(0, 4, 0)
    ring_wait(1, 4, 1)
    far = (z + 4) % NZ
    project_kv((far,), lo)
    project_kv((far,), 1 - lo)
    send_kv((far,))
    project_q((far,), lo)
    project_q((far,), 1 - lo)
    settle(5, 8)
    arrived(wo_half(1 - lo), WY + 2)
    remote(wo_half(1 - lo), wo_half(1 - lo), WSIB + 2, sibling).start()
    prefix_part((far, z))
    prefix_part(around(3))

    def kv_arrive(c, carry):
        for k in (1, 2):
            arrived(kv_chunk(2 - k, c), KVH + 2 * c + k - 1)
        return carry

    lax.fori_loop(0, NZ, kv_arrive, 0)
    arrived(sib_rows(wo, 128), WSIB + 2)

    col_tiles = [pl.ds(n * tile, tile) for n in range(D // tile)]
    suffix_part((far, z))
    out_terms(2)
    for d in range(2):
        for cols in col_tiles:
            sbuf[d, 3, rows_of(d), cols] = tbuf[0, rows_of(d), cols].astype(BF)
        rs_send(d, 4, d)

    def reduce_step(i, carry):
        h = 3 - i

        chunks = around(h)

        @pl.when(i > 0)
        def _():
            prefix_part(chunks)

        suffix_part(chunks)
        out_terms(1)
        for fresh in (True, False):
            for d in range(2):
                p = 1 - d if fresh else d
                if fresh:

                    @pl.when(i > 0)
                    def _():
                        rs_wait(d, h + 1, p)

                else:
                    rs_wait(d, h + 1, p)
                for cols in col_tiles:
                    total = tbuf[d, rows_of(p), cols] + rbuf[d, h, rows_of(p), cols].astype(F32)
                    sbuf[d, h - 1, rows_of(p), cols] = total.astype(BF)
                rs_send(d, h, p)
        return carry

    lax.fori_loop(0, 3, reduce_step, 0)
    for p in range(2):
        for d in range(2):
            rs_wait(d, 1, p)
        for cols in col_tiles:
            total = tbuf[2, rows_of(p), cols] + rbuf[0, 0, rows_of(p), cols].astype(F32)
            out_ref[rows_of(p), cols] = (total + rbuf[1, 0, rows_of(p), cols].astype(F32)).astype(BF)

    left(mine, PZ)
    for k in range(3):
        left(both, PY + k)
    for k in range(2):
        left(x_block(0), PX + k)
        left(x_half(3 - 2 * k, k), PX + 2 + k)
    left(column, PSIB)
    for k, half in enumerate((wq_half, wkv_half, wo_half)):
        left(half(lo), WY + k)
        left(half(1 - lo), WSIB + k)

    def kv_left(c, carry):
        for k in (1, 2):
            left(kv_chunk(2, c), KVH + 2 * c + k - 1)
        return carry

    lax.fori_loop(0, NZ, kv_left, 0)
    for d in range(2):
        for h in range(1, 5):
            for p in range(2):
                if h < 4 or p == d:
                    left(xall.at[0, rows_of(p)], ring_id(RING, d, h, p))
                    left(sbuf.at[d, h - 1, rows_of(p)], ring_id(RS, d, h, p))


def local(x_rows, norm_gain, w_query, w_keyval, w_out, prefix_cache, page_table, request_ids):
    exponents = -(np.arange(HD) % (HD // 2)) * 2.0 / HD
    freqs = jnp.asarray((500000.0**exponents).astype(np.float32)).reshape(1, HD)
    vmem = pl.BlockSpec(memory_space=pltpu.VMEM)
    hbm = pl.BlockSpec(memory_space=pl.ANY)
    return pl.pallas_call(
        kernel,
        out_shape=jax.ShapeDtypeStruct((CH, D), BF),
        in_specs=[vmem] * 5 + [pl.BlockSpec(memory_space=pltpu.SMEM)] + [hbm] * 3,
        out_specs=vmem,
        scratch_shapes=[
            pltpu.VMEM((NZ, CH, D), BF),
            pltpu.VMEM((2, D, 256), BF),
            pltpu.VMEM((2, 128, D), BF),
            pltpu.VMEM((2, 256, D), BF),
            pltpu.VMEM((2, 2, 4, 2, 2, 256, 128), BF),
            pltpu.VMEM((3, 2, 2, HALF, 128), BF),
            pltpu.VMEM((2, NZ, 2 * CH, 256), BF),
            pltpu.VMEM((NZ, 2, 2 * CH, 1), F32),
            pltpu.VMEM((NZ, 2, 2 * CH, 1), F32),
            pltpu.VMEM((NZ, 2, 2 * CH, 256), F32),
            pltpu.VMEM((2 * CH, 512), BF),
            pltpu.VMEM((32, 128), F32),
            pltpu.VMEM((NZ, CH, 1), F32),
            pltpu.VMEM((NZ, CH, HD), F32),
            pltpu.VMEM((NZ, CH, HD), F32),
            pltpu.VMEM((3, CH, D), F32),
            pltpu.VMEM((2, 4, CH, D), BF),
            pltpu.VMEM((2, 4, CH, D), BF),
            pltpu.SemaphoreType.DMA((MESSAGES,)),
            pltpu.SemaphoreType.DMA((MESSAGES,)),
            pltpu.SemaphoreType.DMA((3,)),
        ],
        compiler_params=pltpu.CompilerParams(
            collective_id=0, has_side_effects=True, vmem_limit_bytes=63 << 20
        ),
    )(
        x_rows,
        norm_gain.reshape(1, D),
        prefix_cache.transpose(0, 2, 3, 1).reshape(256, 128),
        request_ids.reshape(128, 128),
        freqs,
        page_table,
        w_query,
        w_keyval.transpose(1, 2, 0).reshape(128, D),
        w_out,
    )


def solution(mesh):
    placed = (
        P(("grp", "tp"), None),
        P(),
        P(None, "tp"),
        P(None, None, "tp"),
        P("tp", None),
        P("grp", None, None, "tp"),
        P(),
        P(),
    )
    return jax.shard_map(
        local, mesh=mesh, in_specs=placed, out_specs=P(("grp", "tp"), None), check_vma=False
    )
```

```python
import math

import jax
import jax.numpy as jnp
import numpy as np
from jax import lax
from jax.experimental import pallas as pl
from jax.experimental.pallas import tpu as pltpu
from jax.sharding import PartitionSpec as P

MESH = pl.DeviceIdType.MESH
HD = 128
SINKS = 4
D = 4096
CH = 64
NZ = 8
HALF = CH * NZ
PREFIX = 4096
SCALE = HD**-0.5 * math.log2(math.e)
NEG = -1e30
BF = jnp.bfloat16
F32 = jnp.float32

RING, PZ, PY, PX, PSIB, WY, WSIB = 0, 16, 17, 20, 24, 25, 28
VZ, VY, VX, VSIB, KVH, RS = 31, 32, 35, 39, 40, 56
MESSAGES = 72


def ring_id(base, d, h, p):
    return base + (d * 4 + (h - 1)) * 2 + p


def kernel(
    x_ref,
    gain_ref,
    pre_ref,
    ids_ref,
    freq_ref,
    pages_ref,
    wq_ref,
    wkv_ref,
    wo_ref,
    out_ref,
    xall,
    wq,
    wkv,
    wv,
    wo,
    px,
    kvs,
    qpad,
    st_m,
    st_l,
    st_acc,
    attn,
    kpe,
    off,
    cosines,
    sines,
    tbuf,
    sbuf,
    rbuf,
    ssem,
    rsem,
    lsem,
):
    g = lax.axis_index("grp")
    t = lax.axis_index("tp")
    core = g % 2
    xx = (g // 2) % 4
    hi = g // 8
    z = t % NZ
    lo = t // NZ
    par = z % 2
    up = (g, lo * NZ + (z + 1) % NZ)
    down = (g, lo * NZ + (z + NZ - 1) % NZ)
    pair = (g, t + 1 - 2 * par)
    other_t = (1 - lo) * NZ + z
    other_g = (1 - hi) * 8 + xx * 2 + core
    sibling = (g + 1 - 2 * core, t)
    weight_peer = (core * other_g + (1 - core) * g, other_t)

    def along_x(k):
        return (hi * 8 + ((xx + k) % 4) * 2 + core, t)

    def half_group(k):
        index = (2 * g + lo + k + 32) % 32
        return (index // 2, (index % 2) * NZ + z)

    def remote(src, dst, number, device):
        return pltpu.make_async_remote_copy(
            src_ref=src,
            dst_ref=dst,
            send_sem=ssem.at[number],
            recv_sem=rsem.at[number],
            device_id=device,
            device_id_type=MESH,
        )

    def arrived(ref, number):
        remote(ref, ref, number, sibling).wait_recv()

    def left(ref, number):
        remote(ref, ref, number, sibling).wait_send()

    ahead = (up, down)
    sign = (1, -1)

    def rows_of(p):
        return pl.ds(p * 32, 32)

    def origin(d, h):
        return (z - sign[d] * h + NZ) % NZ

    partners = [up, down, (g, other_t), (other_g, other_t), (other_g, t)]
    partners += [along_x(1), along_x(3), sibling]
    partners += [half_group(1), half_group(-1), half_group(2), half_group(-2)]
    barrier = pltpu.get_barrier_semaphore()
    for device in partners:
        pl.semaphore_signal(barrier, inc=1, device_id=device, device_id_type=MESH)

    local_wq = pltpu.make_async_copy(wq_ref, wq.at[lo], lsem.at[0])
    local_wkv = pltpu.make_async_copy(wkv_ref, wkv.at[lo], lsem.at[1])
    local_wo = pltpu.make_async_copy(wo_ref, wo.at[lo], lsem.at[2])
    local_wq.start()
    local_wkv.start()
    local_wo.start()
    wide = x_ref[...].astype(F32)
    variance = jnp.mean(wide * wide, axis=-1, keepdims=True) + 1e-05
    xall[z] = (wide * lax.rsqrt(variance) * gain_ref[...]).astype(BF)
    for page in range(2):
        rows = pl.ds(page * 128, 128)
        px[lo, hi, xx, core, par, rows, :] = pre_ref[rows, :].astype(F32).T.astype(BF)
    for d in range(2):
        rbuf[d, 3, rows_of(1 - d)] = jnp.zeros((32, D), BF)

    pl.semaphore_wait(barrier, len(partners))

    local_wkv.wait()
    slice_of_mine = wkv.at[lo, :, pl.ds(pl.multiple_of(g * 256, 256), 256)]
    slice_of_pair = wv.at[lo, hi, xx, core]
    remote(slice_of_mine, slice_of_pair, VZ, pair).start()
    mine = px.at[lo, hi, xx, core, par]
    remote(mine, mine, PZ, pair).start()

    def ring_send(d, h, p):
        block = xall.at[origin(d, h - 1), rows_of(p)]
        remote(block, block, ring_id(RING, d, h, p), ahead[d]).start()

    def ring_wait(d, h, p):
        arrived(xall.at[origin(d, h), rows_of(p)], ring_id(RING, d, h, p))

    for p in range(2):
        for d in range(2):
            ring_send(d, 1, p)

    def wq_half(which):
        return wq.at[which, pl.ds(pl.multiple_of(core * (D // 2), D // 2), D // 2)]

    def wkv_half(which):
        return wkv.at[which, pl.ds(pl.multiple_of(core * 64, 64), 64)]

    def wo_half(which):
        return wo.at[which, pl.ds(pl.multiple_of(core * 128, 128), 128)]

    def sib_rows(ref, size):
        return ref.at[1 - lo, pl.ds(pl.multiple_of((1 - core) * size, size), size)]

    def ring_pass(h, p):
        for d in range(2):
            ring_wait(d, h, p)
            if h < 3 or p == d:
                ring_send(d, h + 1, p)

    lane = lax.broadcasted_iota(jnp.int32, (CH, HD), 1)
    low = lane < HD // 2

    def project_kv(chunks):
        rows = jnp.concatenate([xall[c] for c in chunks], axis=0)
        own = scores_of(rows, jnp.concatenate([wkv[0], wkv[1]], axis=0)).astype(BF).astype(F32)
        other = None
        for k in range(16):
            at = (k // 8, (k // 2) % 4, k % 2)
            weights = jnp.concatenate([wv[(0,) + at], wv[(1,) + at]], axis=0)
            part = scores_of(rows[:, k * 256 : (k + 1) * 256], weights)
            other = part if other is None else other + part
        other = other.astype(BF).astype(F32)
        for n, c in enumerate(chunks):
            cosine = jnp.where(low, cosines[c], 1.0)
            sine = jnp.where(low, -sines[c], 0.0) * turn
            rows_here = pl.ds(pl.multiple_of(c * CH, CH), CH)
            for y in range(2):
                first = own[n * CH : (n + 1) * CH, y * HD : (y + 1) * HD]
                second = other[n * CH : (n + 1) * CH, y * HD : (y + 1) * HD]
                kvs[2, y, par, rows_here] = (first * cosine - second * sine).astype(BF)
                kvs[2, y, 1 - par, rows_here] = (second * cosine + first * sine).astype(BF)

    def project_q(chunks, y):
        rows = jnp.concatenate([xall[c] for c in chunks], axis=0)
        q_part = jnp.dot(rows, wq[y], preferred_element_type=F32)
        for n, c in enumerate(chunks):
            cosine = cosines[c]
            sine = sines[c]
            for head in range(2):
                v = q_part[n * CH : (n + 1) * CH, head * HD : (head + 1) * HD]
                turned = v * cosine + pltpu.roll(v, HD // 2, 1) * sine
                swapped = pltpu.roll(turned, HD // 2, 1)
                first = jnp.where(low, turned, 0.0)
                second = jnp.where(low, swapped, 0.0)
                both_halves = jnp.concatenate([first, second], axis=1).astype(BF)
                qpad[y, c, pl.ds(head * CH, CH), :] = both_halves

    def scores_of(queries, keys):
        return lax.dot_general(queries, keys, (((1,), (1,)), ((), ())), preferred_element_type=F32)

    turn = (1 - 2 * par).astype(F32)

    def kv_chunk(slot, c):
        return kvs.at[slot, :, :, pl.ds(pl.multiple_of(c * CH, CH), CH)]

    def around(h):
        return ((z + h) % NZ, (z + NZ - h) % NZ)

    def project_whole_kv(chunks):
        project_kv(chunks)
        for c in chunks:
            for k in (1, 2):
                remote(kv_chunk(2, c), kv_chunk(2 - k, c), KVH + 2 * c + k - 1, half_group(k)).start()

    pieces = []
    for k in range(3):
        block = 2 * g + lo - 2 + k
        for r in range(4):
            ids = ids_ref[pl.ds(jnp.maximum(block, 0) * 4 + r, 1), :].astype(F32)
            pieces.append(jnp.where(block >= 0, ids, -1.0))
    window = jnp.concatenate(pieces, axis=1)

    def tables(c, carry):
        row = lax.broadcasted_iota(jnp.int32, (CH, 3 * HALF), 0) + c * CH + 2 * HALF
        col = lax.broadcasted_iota(jnp.int32, (CH, 3 * HALF), 1)
        own = jnp.sum(jnp.where(col == row, window, 0.0), axis=1, keepdims=True)
        earlier = (window == own) & (col < row)
        offset = jnp.sum(jnp.where(earlier, 1.0, 0.0), axis=1, keepdims=True)
        off[c] = offset
        angles = (PREFIX + offset) * freq_ref[...]
        sine = jnp.sin(angles)
        cosines[c] = jnp.cos(angles)
        sines[c] = jnp.where(low, -sine, sine)
        return carry

    page_row = lax.broadcasted_iota(jnp.int32, (32, 128), 0)
    logical = jnp.zeros((32, 128), F32)
    for page in range(32):
        logical = logical + jnp.where(page_row == pages_ref[page], float(page), 0.0)
    key_pos = logical * 128.0 + lax.broadcasted_iota(jnp.int32, (32, 128), 1).astype(F32)
    kpe[...] = jnp.where(key_pos < SINKS, 1e6, key_pos)
    def fold(state, queries, keys, visible):
        scores = jnp.where(visible, scores_of(queries, keys), NEG)
        highest = jnp.max(scores, axis=-1, keepdims=True)
        if state is None:
            top = highest
        else:
            top = jnp.maximum(state[0], highest)
        weights = jnp.exp2((scores - top) * SCALE)
        total = jnp.sum(weights, axis=-1, keepdims=True)
        acc = jnp.dot(weights.astype(BF), keys, preferred_element_type=F32)
        if state is None:
            return (top, total, acc)
        factor = jnp.exp2((state[0] - top) * SCALE)
        return (top, state[1] * factor + total, state[2] * factor + acc)

    def pair_queries(chunks, y):
        return jnp.concatenate([qpad[y, c] for c in chunks], axis=0)

    def pair_offsets(chunks):
        return jnp.concatenate([off[c] for c in chunks for _ in range(2)], axis=0)

    def prefix_part(chunks):
        offset = pair_offsets(chunks)
        for y in range(2):
            queries = pair_queries(chunks, y)
            state = None
            for b in range(8):
                parts = []
                for k in range(2):
                    at = (y, b // 4, b % 4, k)
                    parts.append(jnp.concatenate([px[at + (0,)], px[at + (1,)]], axis=1))
                keys = jnp.concatenate(parts, axis=0)
                positions = jnp.concatenate([kpe[pl.ds(4 * b + r, 1), :] for r in range(4)], axis=1)
                state = fold(state, queries, keys, positions > offset)
            for n, c in enumerate(chunks):
                st_m[c, y] = state[0][n * 2 * CH : (n + 1) * 2 * CH]
                st_l[c, y] = state[1][n * 2 * CH : (n + 1) * 2 * CH]
                st_acc[c, y] = state[2][n * 2 * CH : (n + 1) * 2 * CH]

    def suffix_part(chunks):
        offset = pair_offsets(chunks)
        row = lax.broadcasted_iota(jnp.int32, (2 * CH, 1), 0) % CH
        row = jnp.concatenate([row + c * CH for c in chunks], axis=0).astype(F32)
        column_index = lax.broadcasted_iota(jnp.int32, (1, HALF), 1).astype(F32)
        lane2 = lax.broadcasted_iota(jnp.int32, (2 * CH * len(chunks), HD), 1)
        for y in range(2):
            queries = pair_queries(chunks, y)
            state = tuple(
                jnp.concatenate([ref[c, y] for c in chunks], axis=0) for ref in (st_m, st_l, st_acc)
            )
            for slot in range(3):
                keys = jnp.concatenate([kvs[slot, y, 0], kvs[slot, y, 1]], axis=1)
                index = column_index + (slot - 2) * HALF
                visible = (index >= row - offset) & (index <= row)
                state = fold(state, queries, keys, visible)
            result = state[2] / state[1]
            first = pltpu.roll(result[:, :HD], HD // 2, 1)
            merged = jnp.where(lane2 < HD // 2, first, result[:, HD:]).astype(BF)
            for n in range(len(chunks)):
                for head in range(2):
                    part = merged[(2 * n + head) * CH : (2 * n + head + 1) * CH]
                    attn[pl.ds(n * CH, CH), pl.ds(y * 256 + head * HD, HD)] = part

    tile = 1024

    def out_terms(second):
        @pl.loop(0, D // tile)
        def _(n):
            cols = pl.ds(pl.multiple_of(n * tile, tile), tile)
            rows = attn[...]
            term = jnp.dot(rows[:, :256], wo[0, :, cols], preferred_element_type=F32)
            term = term + jnp.dot(rows[:, 256:], wo[1, :, cols], preferred_element_type=F32)
            tbuf[0, :, cols] = term[:CH]
            tbuf[second, :, cols] = term[CH:]

    def rs_send(d, h, p):
        src = sbuf.at[d, h - 1, rows_of(p)]
        dst = rbuf.at[d, h - 1, rows_of(p)]
        remote(src, dst, ring_id(RS, d, h, p), ahead[d]).start()

    def rs_wait(d, h, p):
        arrived(rbuf.at[d, h - 1, rows_of(p)], ring_id(RS, d, h, p))

    def x_block(k):
        return px.at[:, :, (xx + k) % 4, core]

    def x_half(k, which):
        return px.at[:, :, (xx + k) % 4, core, which]

    y_side = ((g, other_t), (other_g, other_t), (other_g, t))
    arrived(slice_of_pair, VZ)
    for k in range(3):
        remote(slice_of_pair, slice_of_pair, VY + k, y_side[k]).start()
    arrived(px.at[lo, hi, xx, core, 1 - par], PZ)
    both = px.at[lo, hi, xx, core]
    for k in range(3):
        remote(both, both, PY + k, y_side[k]).start()
    remote(wkv_half(lo), wkv_half(lo), WY + 1, weight_peer).start()
    local_wq.wait()
    remote(wq_half(lo), wq_half(lo), WY, weight_peer).start()
    from_y = ((1 - lo, hi), (1 - lo, 1 - hi), (lo, 1 - hi))
    for k in range(3):
        arrived(wv.at[from_y[k][0], from_y[k][1], xx, core], VY + k)

    def v_block(k):
        return wv.at[:, :, (xx + k) % 4, core]

    def v_half(k, which):
        return wv.at[which, :, (xx + k) % 4, core]

    remote(v_block(0), v_block(0), VX, along_x(1)).start()
    remote(v_block(0), v_block(0), VX + 1, along_x(3)).start()
    lax.fori_loop(0, NZ, tables, 0)
    for k in range(3):
        arrived(px.at[from_y[k][0], from_y[k][1], xx, core], PY + k)
    project_q((z,), lo)
    ring_pass(1, 0)
    arrived(v_block(3), VX)
    remote(v_half(3, 0), v_half(3, 0), VX + 2, along_x(1)).start()
    arrived(v_block(1), VX + 1)
    remote(v_half(1, 1), v_half(1, 1), VX + 3, along_x(3)).start()
    remote(x_block(0), x_block(0), PX, along_x(1)).start()
    remote(x_block(0), x_block(0), PX + 1, along_x(3)).start()
    ring_pass(1, 1)
    arrived(v_half(2, 0), VX + 2)
    arrived(v_half(2, 1), VX + 3)
    v_column = wv.at[:, :, :, core]
    remote(v_column, v_column, VSIB, sibling).start()
    arrived(wkv_half(1 - lo), WY + 1)
    remote(wkv_half(1 - lo), wkv_half(1 - lo), WSIB + 1, sibling).start()
    project_q(around(1), lo)
    ring_pass(2, 0)
    arrived(wv.at[:, :, :, 1 - core], VSIB)
    arrived(sib_rows(wkv, 64), WSIB + 1)
    project_whole_kv((z,))
    project_whole_kv(around(1))
    ring_pass(2, 1)
    arrived(x_block(3), PX)
    remote(x_half(3, 0), x_half(3, 0), PX + 2, along_x(1)).start()
    arrived(x_block(1), PX + 1)
    remote(x_half(1, 1), x_half(1, 1), PX + 3, along_x(3)).start()
    arrived(wq_half(1 - lo), WY)
    remote(wq_half(1 - lo), wq_half(1 - lo), WSIB, sibling).start()
    project_whole_kv(around(2))
    ring_pass(3, 0)
    local_wo.wait()
    remote(wo_half(lo), wo_half(lo), WY + 2, weight_peer).start()
    project_q(around(2), lo)
    arrived(sib_rows(wq, D // 2), WSIB)
    project_q((z,), 1 - lo)
    project_q(around(1), 1 - lo)
    arrived(x_half(2, 0), PX + 2)
    arrived(x_half(2, 1), PX + 3)
    column = px.at[:, :, :, core]
    remote(column, column, PSIB, sibling).start()
    ring_pass(3, 1)
    project_whole_kv(around(3))
    project_q(around(3), lo)
    project_q(around(3), 1 - lo)
    arrived(px.at[:, :, :, 1 - core], PSIB)
    prefix_part(around(3))
    ring_wait(0, 4, 0)
    ring_wait(1, 4, 1)
    far = (z + 4) % NZ
    project_whole_kv((far,))
    project_q((far,), lo)
    project_q((far,), 1 - lo)
    prefix_part((far, z))
    arrived(wo_half(1 - lo), WY + 2)
    remote(wo_half(1 - lo), wo_half(1 - lo), WSIB + 2, sibling).start()
    def kv_arrive(c, carry):
        for k in (1, 2):
            arrived(kv_chunk(2 - k, c), KVH + 2 * c + k - 1)
        return carry

    lax.fori_loop(0, NZ, kv_arrive, 0)
    arrived(sib_rows(wo, 128), WSIB + 2)

    col_tiles = [pl.ds(n * tile, tile) for n in range(D // tile)]
    suffix_part((far, z))
    out_terms(2)
    for d in range(2):
        for cols in col_tiles:
            sbuf[d, 3, rows_of(d), cols] = tbuf[0, rows_of(d), cols].astype(BF)
        rs_send(d, 4, d)
    project_q(around(2), 1 - lo)

    def reduce_step(i, carry):
        h = 3 - i

        chunks = around(h)

        @pl.when(i > 0)
        def _():
            prefix_part(chunks)

        suffix_part(chunks)
        out_terms(1)
        for fresh in (True, False):
            for d in range(2):
                p = 1 - d if fresh else d
                if fresh:

                    @pl.when(i > 0)
                    def _():
                        rs_wait(d, h + 1, p)

                else:
                    rs_wait(d, h + 1, p)
                for cols in col_tiles:
                    total = tbuf[d, rows_of(p), cols] + rbuf[d, h, rows_of(p), cols].astype(F32)
                    sbuf[d, h - 1, rows_of(p), cols] = total.astype(BF)
                rs_send(d, h, p)
        return carry

    lax.fori_loop(0, 3, reduce_step, 0)
    for p in range(2):
        for d in range(2):
            rs_wait(d, 1, p)
        for cols in col_tiles:
            total = tbuf[2, rows_of(p), cols] + rbuf[0, 0, rows_of(p), cols].astype(F32)
            out_ref[rows_of(p), cols] = (total + rbuf[1, 0, rows_of(p), cols].astype(F32)).astype(BF)

    left(mine, PZ)
    for k in range(3):
        left(both, PY + k)
        left(slice_of_pair, VY + k)
    for k in range(2):
        left(x_block(0), PX + k)
        left(x_half(3 - 2 * k, k), PX + 2 + k)
        left(v_block(0), VX + k)
        left(v_half(3 - 2 * k, k), VX + 2 + k)
    left(column, PSIB)
    left(slice_of_mine, VZ)
    left(v_column, VSIB)
    for k, half in enumerate((wq_half, wkv_half, wo_half)):
        left(half(lo), WY + k)
        left(half(1 - lo), WSIB + k)

    def kv_left(c, carry):
        for k in (1, 2):
            left(kv_chunk(2, c), KVH + 2 * c + k - 1)
        return carry

    lax.fori_loop(0, NZ, kv_left, 0)
    for d in range(2):
        for h in range(1, 5):
            for p in range(2):
                if h < 4 or p == d:
                    left(xall.at[0, rows_of(p)], ring_id(RING, d, h, p))
                    left(sbuf.at[d, h - 1, rows_of(p)], ring_id(RS, d, h, p))


def local(x_rows, norm_gain, w_query, w_keyval, w_out, prefix_cache, page_table, request_ids):
    exponents = -(np.arange(HD) % (HD // 2)) * 2.0 / HD
    freqs = jnp.asarray((500000.0**exponents).astype(np.float32)).reshape(1, HD)
    vmem = pl.BlockSpec(memory_space=pltpu.VMEM)
    hbm = pl.BlockSpec(memory_space=pl.ANY)
    return pl.pallas_call(
        kernel,
        out_shape=jax.ShapeDtypeStruct((CH, D), BF),
        in_specs=[vmem] * 5 + [pl.BlockSpec(memory_space=pltpu.SMEM)] + [hbm] * 3,
        out_specs=vmem,
        scratch_shapes=[
            pltpu.VMEM((NZ, CH, D), BF),
            pltpu.VMEM((2, D, 256), BF),
            pltpu.VMEM((2, 128, D), BF),
            pltpu.VMEM((2, 2, 4, 2, 128, 256), BF),
            pltpu.VMEM((2, 256, D), BF),
            pltpu.VMEM((2, 2, 4, 2, 2, 256, 128), BF),
            pltpu.VMEM((3, 2, 2, HALF, 128), BF),
            pltpu.VMEM((2, NZ, 2 * CH, 256), BF),
            pltpu.VMEM((NZ, 2, 2 * CH, 1), F32),
            pltpu.VMEM((NZ, 2, 2 * CH, 1), F32),
            pltpu.VMEM((NZ, 2, 2 * CH, 256), F32),
            pltpu.VMEM((2 * CH, 512), BF),
            pltpu.VMEM((32, 128), F32),
            pltpu.VMEM((NZ, CH, 1), F32),
            pltpu.VMEM((NZ, CH, HD), F32),
            pltpu.VMEM((NZ, CH, HD), F32),
            pltpu.VMEM((3, CH, D), F32),
            pltpu.VMEM((2, 4, CH, D), BF),
            pltpu.VMEM((2, 4, CH, D), BF),
            pltpu.SemaphoreType.DMA((MESSAGES,)),
            pltpu.SemaphoreType.DMA((MESSAGES,)),
            pltpu.SemaphoreType.DMA((3,)),
        ],
        compiler_params=pltpu.CompilerParams(
            collective_id=0, has_side_effects=True, vmem_limit_bytes=63 << 20
        ),
    )(
        x_rows,
        norm_gain.reshape(1, D),
        prefix_cache.transpose(0, 2, 3, 1).reshape(256, 128),
        request_ids.reshape(128, 128),
        freqs,
        page_table,
        w_query,
        w_keyval.transpose(1, 2, 0).reshape(128, D),
        w_out,
    )


def solution(mesh):
    placed = (
        P(("grp", "tp"), None),
        P(),
        P(None, "tp"),
        P(None, None, "tp"),
        P("tp", None),
        P("grp", None, None, "tp"),
        P(),
        P(),
    )
    return jax.shard_map(
        local, mesh=mesh, in_specs=placed, out_specs=P(("grp", "tp"), None), check_vma=False
    )
```

```python
import math

import jax
import jax.numpy as jnp
import numpy as np
from jax import lax
from jax.experimental import pallas as pl
from jax.experimental.pallas import tpu as pltpu
from jax.sharding import PartitionSpec as P

MESH = pl.DeviceIdType.MESH
HD = 128
SINKS = 4
D = 4096
CH = 64
NZ = 8
HALF = CH * NZ
PREFIX = 4096
SCALE = HD**-0.5 * math.log2(math.e)
NEG = -1e30
BF = jnp.bfloat16
F32 = jnp.float32

RING, PZ, PY, PX, PSIB, WY, WSIB = 0, 16, 17, 20, 24, 25, 28
VZ, VY, VX, VSIB, KVH, RS = 31, 32, 35, 39, 40, 56
MESSAGES = 72


def ring_id(base, d, h, p):
    return base + (d * 4 + (h - 1)) * 2 + p


def kernel(
    x_ref,
    gain_ref,
    pre_ref,
    ids_ref,
    freq_ref,
    pages_ref,
    wq_ref,
    wkv_ref,
    wo_ref,
    out_ref,
    xall,
    wq,
    wkv,
    wv,
    wo,
    px,
    kvs,
    qpad,
    st_m,
    st_l,
    st_acc,
    attn,
    kpe,
    off,
    cosines,
    sines,
    tbuf,
    sbuf,
    rbuf,
    ssem,
    rsem,
    lsem,
):
    g = lax.axis_index("grp")
    t = lax.axis_index("tp")
    core = g % 2
    xx = (g // 2) % 4
    hi = g // 8
    z = t % NZ
    lo = t // NZ
    par = z % 2
    up = (g, lo * NZ + (z + 1) % NZ)
    down = (g, lo * NZ + (z + NZ - 1) % NZ)
    pair = (g, t + 1 - 2 * par)
    other_t = (1 - lo) * NZ + z
    other_g = (1 - hi) * 8 + xx * 2 + core
    sibling = (g + 1 - 2 * core, t)
    weight_peer = (core * other_g + (1 - core) * g, other_t)

    def along_x(k):
        return (hi * 8 + ((xx + k) % 4) * 2 + core, t)

    def half_group(k):
        index = (2 * g + lo + k + 32) % 32
        return (index // 2, (index % 2) * NZ + z)

    def remote(src, dst, number, device):
        return pltpu.make_async_remote_copy(
            src_ref=src,
            dst_ref=dst,
            send_sem=ssem.at[number],
            recv_sem=rsem.at[number],
            device_id=device,
            device_id_type=MESH,
        )

    def arrived(ref, number):
        remote(ref, ref, number, sibling).wait_recv()

    def left(ref, number):
        remote(ref, ref, number, sibling).wait_send()

    ahead = (up, down)
    sign = (1, -1)

    def rows_of(p):
        return pl.ds(p * 32, 32)

    def origin(d, h):
        return (z - sign[d] * h + NZ) % NZ

    partners = [up, down, (g, other_t), (other_g, other_t), (other_g, t)]
    partners += [along_x(1), along_x(3), sibling]
    partners += [half_group(1), half_group(-1), half_group(2), half_group(-2)]
    barrier = pltpu.get_barrier_semaphore()
    for device in partners:
        pl.semaphore_signal(barrier, inc=1, device_id=device, device_id_type=MESH)

    local_wq = pltpu.make_async_copy(wq_ref, wq.at[lo], lsem.at[0])
    local_wkv = pltpu.make_async_copy(wkv_ref, wkv.at[lo], lsem.at[1])
    local_wo = pltpu.make_async_copy(wo_ref, wo.at[lo], lsem.at[2])
    local_wq.start()
    local_wkv.start()
    local_wo.start()
    wide = x_ref[...].astype(F32)
    variance = jnp.mean(wide * wide, axis=-1, keepdims=True) + 1e-05
    xall[z] = (wide * lax.rsqrt(variance) * gain_ref[...]).astype(BF)
    for page in range(2):
        rows = pl.ds(page * 128, 128)
        px[lo, hi, xx, core, par, rows, :] = pre_ref[rows, :].astype(F32).T.astype(BF)
    for d in range(2):
        rbuf[d, 3, rows_of(1 - d)] = jnp.zeros((32, D), BF)

    pl.semaphore_wait(barrier, len(partners))

    local_wkv.wait()
    slice_of_mine = wkv.at[lo, :, pl.ds(pl.multiple_of(g * 256, 256), 256)]
    slice_of_pair = wv.at[lo, hi, xx, core]
    remote(slice_of_mine, slice_of_pair, VZ, pair).start()
    mine = px.at[lo, hi, xx, core, par]
    remote(mine, mine, PZ, pair).start()

    def ring_send(d, h, p):
        block = xall.at[origin(d, h - 1), rows_of(p)]
        remote(block, block, ring_id(RING, d, h, p), ahead[d]).start()

    def ring_wait(d, h, p):
        arrived(xall.at[origin(d, h), rows_of(p)], ring_id(RING, d, h, p))

    for p in range(2):
        for d in range(2):
            ring_send(d, 1, p)

    def wq_half(which):
        return wq.at[which, pl.ds(pl.multiple_of(core * (D // 2), D // 2), D // 2)]

    def wkv_half(which):
        return wkv.at[which, pl.ds(pl.multiple_of(core * 64, 64), 64)]

    def wo_half(which):
        return wo.at[which, pl.ds(pl.multiple_of(core * 128, 128), 128)]

    def sib_rows(ref, size):
        return ref.at[1 - lo, pl.ds(pl.multiple_of((1 - core) * size, size), size)]

    def ring_pass(h, p):
        for d in range(2):
            ring_wait(d, h, p)
            if h < 3 or p == d:
                ring_send(d, h + 1, p)

    lane = lax.broadcasted_iota(jnp.int32, (CH, HD), 1)
    low = lane < HD // 2

    def project_kv(chunks):
        rows = jnp.concatenate([xall[c] for c in chunks], axis=0)
        own = scores_of(rows, jnp.concatenate([wkv[0], wkv[1]], axis=0)).astype(BF).astype(F32)
        other = None
        for k in range(16):
            at = (k // 8, (k // 2) % 4, k % 2)
            weights = jnp.concatenate([wv[(0,) + at], wv[(1,) + at]], axis=0)
            part = scores_of(rows[:, k * 256 : (k + 1) * 256], weights)
            other = part if other is None else other + part
        other = other.astype(BF).astype(F32)
        for n, c in enumerate(chunks):
            cosine = jnp.where(low, cosines[c], 1.0)
            sine = jnp.where(low, -sines[c], 0.0) * turn
            rows_here = pl.ds(pl.multiple_of(c * CH, CH), CH)
            for y in range(2):
                first = own[n * CH : (n + 1) * CH, y * HD : (y + 1) * HD]
                second = other[n * CH : (n + 1) * CH, y * HD : (y + 1) * HD]
                kvs[2, y, par, rows_here] = (first * cosine - second * sine).astype(BF)
                kvs[2, y, 1 - par, rows_here] = (second * cosine + first * sine).astype(BF)

    def project_q(chunks, y):
        rows = jnp.concatenate([xall[c] for c in chunks], axis=0)
        q_part = jnp.dot(rows, wq[y], preferred_element_type=F32)
        for n, c in enumerate(chunks):
            cosine = cosines[c]
            sine = sines[c]
            for head in range(2):
                v = q_part[n * CH : (n + 1) * CH, head * HD : (head + 1) * HD]
                turned = v * cosine + pltpu.roll(v, HD // 2, 1) * sine
                swapped = pltpu.roll(turned, HD // 2, 1)
                first = jnp.where(low, turned, 0.0)
                second = jnp.where(low, swapped, 0.0)
                both_halves = jnp.concatenate([first, second], axis=1).astype(BF)
                qpad[y, c, pl.ds(head * CH, CH), :] = both_halves

    def scores_of(queries, keys):
        return lax.dot_general(queries, keys, (((1,), (1,)), ((), ())), preferred_element_type=F32)

    turn = (1 - 2 * par).astype(F32)

    def kv_chunk(slot, c):
        return kvs.at[slot, :, :, pl.ds(pl.multiple_of(c * CH, CH), CH)]

    def around(h):
        return ((z + h) % NZ, (z + NZ - h) % NZ)

    def project_whole_kv(chunks):
        project_kv(chunks)
        for c in chunks:
            for k in (1, 2):
                remote(kv_chunk(2, c), kv_chunk(2 - k, c), KVH + 2 * c + k - 1, half_group(k)).start()

    pieces = []
    for k in range(3):
        block = 2 * g + lo - 2 + k
        for r in range(4):
            ids = ids_ref[pl.ds(jnp.maximum(block, 0) * 4 + r, 1), :].astype(F32)
            pieces.append(jnp.where(block >= 0, ids, -1.0))
    window = jnp.concatenate(pieces, axis=1)

    def tables(c, carry):
        row = lax.broadcasted_iota(jnp.int32, (CH, 3 * HALF), 0) + c * CH + 2 * HALF
        col = lax.broadcasted_iota(jnp.int32, (CH, 3 * HALF), 1)
        own = jnp.sum(jnp.where(col == row, window, 0.0), axis=1, keepdims=True)
        earlier = (window == own) & (col < row)
        offset = jnp.sum(jnp.where(earlier, 1.0, 0.0), axis=1, keepdims=True)
        off[c] = offset
        angles = (PREFIX + offset) * freq_ref[...]
        sine = jnp.sin(angles)
        cosines[c] = jnp.cos(angles)
        sines[c] = jnp.where(low, -sine, sine)
        return carry

    page_row = lax.broadcasted_iota(jnp.int32, (32, 128), 0)
    logical = jnp.zeros((32, 128), F32)
    for page in range(32):
        logical = logical + jnp.where(page_row == pages_ref[page], float(page), 0.0)
    key_pos = logical * 128.0 + lax.broadcasted_iota(jnp.int32, (32, 128), 1).astype(F32)
    kpe[...] = jnp.where(key_pos < SINKS, 1e6, key_pos)
    def fold(state, queries, keys, visible):
        scores = jnp.where(visible, scores_of(queries, keys), NEG)
        highest = jnp.max(scores, axis=-1, keepdims=True)
        if state is None:
            top = highest
        else:
            top = jnp.maximum(state[0], highest)
        weights = jnp.exp2((scores - top) * SCALE)
        total = jnp.sum(weights, axis=-1, keepdims=True)
        acc = jnp.dot(weights.astype(BF), keys, preferred_element_type=F32)
        if state is None:
            return (top, total, acc)
        factor = jnp.exp2((state[0] - top) * SCALE)
        return (top, state[1] * factor + total, state[2] * factor + acc)

    def pair_queries(chunks, y):
        return jnp.concatenate([qpad[y, c] for c in chunks], axis=0)

    def pair_offsets(chunks):
        return jnp.concatenate([off[c] for c in chunks for _ in range(2)], axis=0)

    def prefix_part(chunks, heads=(0, 1)):
        offset = pair_offsets(chunks)
        for y in heads:
            queries = pair_queries(chunks, y)
            state = None
            for b in range(8):
                parts = []
                for k in range(2):
                    at = (y, b // 4, b % 4, k)
                    parts.append(jnp.concatenate([px[at + (0,)], px[at + (1,)]], axis=1))
                keys = jnp.concatenate(parts, axis=0)
                positions = jnp.concatenate([kpe[pl.ds(4 * b + r, 1), :] for r in range(4)], axis=1)
                state = fold(state, queries, keys, positions > offset)
            for n, c in enumerate(chunks):
                st_m[c, y] = state[0][n * 2 * CH : (n + 1) * 2 * CH]
                st_l[c, y] = state[1][n * 2 * CH : (n + 1) * 2 * CH]
                st_acc[c, y] = state[2][n * 2 * CH : (n + 1) * 2 * CH]

    def suffix_part(chunks):
        offset = pair_offsets(chunks)
        row = lax.broadcasted_iota(jnp.int32, (2 * CH, 1), 0) % CH
        row = jnp.concatenate([row + c * CH for c in chunks], axis=0).astype(F32)
        column_index = lax.broadcasted_iota(jnp.int32, (1, HALF), 1).astype(F32)
        lane2 = lax.broadcasted_iota(jnp.int32, (2 * CH * len(chunks), HD), 1)
        for y in range(2):
            queries = pair_queries(chunks, y)
            state = tuple(
                jnp.concatenate([ref[c, y] for c in chunks], axis=0) for ref in (st_m, st_l, st_acc)
            )
            for slot in range(3):
                keys = jnp.concatenate([kvs[slot, y, 0], kvs[slot, y, 1]], axis=1)
                index = column_index + (slot - 2) * HALF
                visible = (index >= row - offset) & (index <= row)
                state = fold(state, queries, keys, visible)
            result = state[2] / state[1]
            first = pltpu.roll(result[:, :HD], HD // 2, 1)
            merged = jnp.where(lane2 < HD // 2, first, result[:, HD:]).astype(BF)
            for n in range(len(chunks)):
                for head in range(2):
                    part = merged[(2 * n + head) * CH : (2 * n + head + 1) * CH]
                    attn[pl.ds(n * CH, CH), pl.ds(y * 256 + head * HD, HD)] = part

    tile = 1024

    def out_terms(second):
        @pl.loop(0, D // tile)
        def _(n):
            cols = pl.ds(pl.multiple_of(n * tile, tile), tile)
            rows = attn[...]
            term = jnp.dot(rows[:, :256], wo[0, :, cols], preferred_element_type=F32)
            term = term + jnp.dot(rows[:, 256:], wo[1, :, cols], preferred_element_type=F32)
            tbuf[0, :, cols] = term[:CH]
            tbuf[second, :, cols] = term[CH:]

    def rs_send(d, h, p):
        src = sbuf.at[d, h - 1, rows_of(p)]
        dst = rbuf.at[d, h - 1, rows_of(p)]
        remote(src, dst, ring_id(RS, d, h, p), ahead[d]).start()

    def rs_wait(d, h, p):
        arrived(rbuf.at[d, h - 1, rows_of(p)], ring_id(RS, d, h, p))

    def x_block(k):
        return px.at[:, :, (xx + k) % 4, core]

    def x_half(k, which):
        return px.at[:, :, (xx + k) % 4, core, which]

    y_side = ((g, other_t), (other_g, other_t), (other_g, t))
    arrived(slice_of_pair, VZ)
    for k in range(3):
        remote(slice_of_pair, slice_of_pair, VY + k, y_side[k]).start()
    arrived(px.at[lo, hi, xx, core, 1 - par], PZ)
    both = px.at[lo, hi, xx, core]
    for k in range(3):
        remote(both, both, PY + k, y_side[k]).start()
    remote(wkv_half(lo), wkv_half(lo), WY + 1, weight_peer).start()
    local_wq.wait()
    remote(wq_half(lo), wq_half(lo), WY, weight_peer).start()
    from_y = ((1 - lo, hi), (1 - lo, 1 - hi), (lo, 1 - hi))
    for k in range(3):
        arrived(wv.at[from_y[k][0], from_y[k][1], xx, core], VY + k)

    def v_block(k):
        return wv.at[:, :, (xx + k) % 4, core]

    def v_half(k, which):
        return wv.at[which, :, (xx + k) % 4, core]

    remote(v_block(0), v_block(0), VX, along_x(1)).start()
    remote(v_block(0), v_block(0), VX + 1, along_x(3)).start()
    lax.fori_loop(0, NZ, tables, 0)
    for k in range(3):
        arrived(px.at[from_y[k][0], from_y[k][1], xx, core], PY + k)
    project_q((z,), lo)
    ring_pass(1, 0)
    arrived(v_block(3), VX)
    remote(v_half(3, 0), v_half(3, 0), VX + 2, along_x(1)).start()
    arrived(v_block(1), VX + 1)
    remote(v_half(1, 1), v_half(1, 1), VX + 3, along_x(3)).start()
    remote(x_block(0), x_block(0), PX, along_x(1)).start()
    remote(x_block(0), x_block(0), PX + 1, along_x(3)).start()
    ring_pass(1, 1)
    arrived(v_half(2, 0), VX + 2)
    arrived(v_half(2, 1), VX + 3)
    v_column = wv.at[:, :, :, core]
    remote(v_column, v_column, VSIB, sibling).start()
    arrived(wkv_half(1 - lo), WY + 1)
    remote(wkv_half(1 - lo), wkv_half(1 - lo), WSIB + 1, sibling).start()
    project_q(around(1), lo)
    ring_pass(2, 0)
    arrived(wv.at[:, :, :, 1 - core], VSIB)
    arrived(sib_rows(wkv, 64), WSIB + 1)
    project_whole_kv((z,))
    project_whole_kv(around(1))
    ring_pass(2, 1)
    arrived(x_block(3), PX)
    remote(x_half(3, 0), x_half(3, 0), PX + 2, along_x(1)).start()
    arrived(x_block(1), PX + 1)
    remote(x_half(1, 1), x_half(1, 1), PX + 3, along_x(3)).start()
    arrived(wq_half(1 - lo), WY)
    remote(wq_half(1 - lo), wq_half(1 - lo), WSIB, sibling).start()
    project_whole_kv(around(2))
    ring_pass(3, 0)
    local_wo.wait()
    remote(wo_half(lo), wo_half(lo), WY + 2, weight_peer).start()
    project_q(around(2), lo)
    arrived(sib_rows(wq, D // 2), WSIB)
    project_q((z,), 1 - lo)
    project_q(around(1), 1 - lo)
    arrived(x_half(2, 0), PX + 2)
    arrived(x_half(2, 1), PX + 3)
    column = px.at[:, :, :, core]
    remote(column, column, PSIB, sibling).start()
    ring_pass(3, 1)
    project_whole_kv(around(3))
    project_q(around(3), lo)
    project_q(around(3), 1 - lo)
    arrived(px.at[:, :, :, 1 - core], PSIB)
    prefix_part(around(3))
    ring_wait(0, 4, 0)
    ring_wait(1, 4, 1)
    far = (z + 4) % NZ
    project_whole_kv((far,))
    project_q((far,), lo)
    project_q((far,), 1 - lo)
    prefix_part((far, z), (0,))
    arrived(wo_half(1 - lo), WY + 2)
    remote(wo_half(1 - lo), wo_half(1 - lo), WSIB + 2, sibling).start()
    prefix_part((far, z), (1,))
    def kv_arrive(c, carry):
        for k in (1, 2):
            arrived(kv_chunk(2 - k, c), KVH + 2 * c + k - 1)
        return carry

    lax.fori_loop(0, NZ, kv_arrive, 0)

    col_tiles = [pl.ds(n * tile, tile) for n in range(D // tile)]
    suffix_part((far, z))
    arrived(sib_rows(wo, 128), WSIB + 2)
    out_terms(2)
    for d in range(2):
        for cols in col_tiles:
            sbuf[d, 3, rows_of(d), cols] = tbuf[0, rows_of(d), cols].astype(BF)
        rs_send(d, 4, d)
    project_q(around(2), 1 - lo)

    def reduce_step(i, carry):
        h = 3 - i

        chunks = around(h)

        @pl.when(i > 0)
        def _():
            prefix_part(chunks)

        suffix_part(chunks)
        out_terms(1)
        for fresh in (True, False):
            for d in range(2):
                p = 1 - d if fresh else d
                if fresh:

                    @pl.when(i > 0)
                    def _():
                        rs_wait(d, h + 1, p)

                else:
                    rs_wait(d, h + 1, p)
                for cols in col_tiles:
                    total = tbuf[d, rows_of(p), cols] + rbuf[d, h, rows_of(p), cols].astype(F32)
                    sbuf[d, h - 1, rows_of(p), cols] = total.astype(BF)
                rs_send(d, h, p)
        return carry

    lax.fori_loop(0, 3, reduce_step, 0)
    for p in range(2):
        for d in range(2):
            rs_wait(d, 1, p)
        for cols in col_tiles:
            total = tbuf[2, rows_of(p), cols] + rbuf[0, 0, rows_of(p), cols].astype(F32)
            out_ref[rows_of(p), cols] = (total + rbuf[1, 0, rows_of(p), cols].astype(F32)).astype(BF)

    left(mine, PZ)
    for k in range(3):
        left(both, PY + k)
        left(slice_of_pair, VY + k)
    for k in range(2):
        left(x_block(0), PX + k)
        left(x_half(3 - 2 * k, k), PX + 2 + k)
        left(v_block(0), VX + k)
        left(v_half(3 - 2 * k, k), VX + 2 + k)
    left(column, PSIB)
    left(slice_of_mine, VZ)
    left(v_column, VSIB)
    for k, half in enumerate((wq_half, wkv_half, wo_half)):
        left(half(lo), WY + k)
        left(half(1 - lo), WSIB + k)

    def kv_left(c, carry):
        for k in (1, 2):
            left(kv_chunk(2, c), KVH + 2 * c + k - 1)
        return carry

    lax.fori_loop(0, NZ, kv_left, 0)
    for d in range(2):
        for h in range(1, 5):
            for p in range(2):
                if h < 4 or p == d:
                    left(xall.at[0, rows_of(p)], ring_id(RING, d, h, p))
                    left(sbuf.at[d, h - 1, rows_of(p)], ring_id(RS, d, h, p))


def local(x_rows, norm_gain, w_query, w_keyval, w_out, prefix_cache, page_table, request_ids):
    exponents = -(np.arange(HD) % (HD // 2)) * 2.0 / HD
    freqs = jnp.asarray((500000.0**exponents).astype(np.float32)).reshape(1, HD)
    vmem = pl.BlockSpec(memory_space=pltpu.VMEM)
    hbm = pl.BlockSpec(memory_space=pl.ANY)
    return pl.pallas_call(
        kernel,
        out_shape=jax.ShapeDtypeStruct((CH, D), BF),
        in_specs=[vmem] * 5 + [pl.BlockSpec(memory_space=pltpu.SMEM)] + [hbm] * 3,
        out_specs=vmem,
        scratch_shapes=[
            pltpu.VMEM((NZ, CH, D), BF),
            pltpu.VMEM((2, D, 256), BF),
            pltpu.VMEM((2, 128, D), BF),
            pltpu.VMEM((2, 2, 4, 2, 128, 256), BF),
            pltpu.VMEM((2, 256, D), BF),
            pltpu.VMEM((2, 2, 4, 2, 2, 256, 128), BF),
            pltpu.VMEM((3, 2, 2, HALF, 128), BF),
            pltpu.VMEM((2, NZ, 2 * CH, 256), BF),
            pltpu.VMEM((NZ, 2, 2 * CH, 1), F32),
            pltpu.VMEM((NZ, 2, 2 * CH, 1), F32),
            pltpu.VMEM((NZ, 2, 2 * CH, 256), F32),
            pltpu.VMEM((2 * CH, 512), BF),
            pltpu.VMEM((32, 128), F32),
            pltpu.VMEM((NZ, CH, 1), F32),
            pltpu.VMEM((NZ, CH, HD), F32),
            pltpu.VMEM((NZ, CH, HD), F32),
            pltpu.VMEM((3, CH, D), F32),
            pltpu.VMEM((2, 4, CH, D), BF),
            pltpu.VMEM((2, 4, CH, D), BF),
            pltpu.SemaphoreType.DMA((MESSAGES,)),
            pltpu.SemaphoreType.DMA((MESSAGES,)),
            pltpu.SemaphoreType.DMA((3,)),
        ],
        compiler_params=pltpu.CompilerParams(
            collective_id=0, has_side_effects=True, vmem_limit_bytes=63 << 20
        ),
    )(
        x_rows,
        norm_gain.reshape(1, D),
        prefix_cache.transpose(0, 2, 3, 1).reshape(256, 128),
        request_ids.reshape(128, 128),
        freqs,
        page_table,
        w_query,
        w_keyval.transpose(1, 2, 0).reshape(128, D),
        w_out,
    )


def solution(mesh):
    placed = (
        P(("grp", "tp"), None),
        P(),
        P(None, "tp"),
        P(None, None, "tp"),
        P("tp", None),
        P("grp", None, None, "tp"),
        P(),
        P(),
    )
    return jax.shard_map(
        local, mesh=mesh, in_specs=placed, out_specs=P(("grp", "tp"), None), check_vma=False
    )
```
